32 devices in a mesh: head: 4 (over x, core), seq: 8 (over z, y).
Axes of the slice: x: 2, y: 2, z: 4, core: 2. Of those that a mesh axis runs over, the one named last changes fastest.
Arguments:
- queries: bfloat16 [12288, 4096], P('seq', 'head'), may hold values from -32 to 32
- key_rows: bfloat16 [12288, 4096], P('seq', 'head'), may hold values from -32 to 32
- value_rows: bfloat16 [12288, 4096], P('seq', 'head'), may hold values from -6 to 6
- learn_rates: bfloat16 [12288, 8], P('seq', 'head'), may hold values from 0.00025367737 to 0.0025482178
- gate_fast: float32 [8, 512, 512], P('head'), may hold values from -0.25 to 0.25
- down_fast: float32 [8, 512, 512], P('head'), may hold values from -0.25 to 0.25
- up_fast: float32 [8, 512, 512], P('head'), may hold values from -0.25 to 0.25
Outputs:
- mixed: bfloat16 [12288, 4096], P('seq', 'head')
The draws below stay inside these ranges and needn't reach their ends.
All inputs are finite; a program needn't handle non-finite values.
Results may differ from the reference program's by a relative error of at most 0.024.
Values may be sent and summed in bfloat16 or wider, within the bound.
No kernel may reach another device: no remote copies, remote signals or barrier semaphores. Data moves between devices by JAX's collectives and lax.ppermute only.
A program may use at most 128 MiB of HBM per device.

```python
import math
import jax
import jax.numpy as jnp
from jax import lax

H = 8
DH = 512
AH = 128
WINDOW = 512
D = 4096
TOKENS = 12288
GROUP = 6144


def paired_rows(key):
    base_key = jax.random.fold_in(key, 4242)
    first_key, second_key = jax.random.split(base_key, 2)
    query_all = jax.random.truncated_normal(first_key, -4.0, 4.0, (TOKENS, D), jnp.float32)
    key_all = jax.random.truncated_normal(second_key, -4.0, 4.0, (TOKENS, D), jnp.float32)
    return (query_all, key_all)


def draw_queries(key, part):
    return paired_rows(key)[0].astype(jnp.bfloat16)


def draw_key_rows(key, part):
    return paired_rows(key)[1].astype(jnp.bfloat16)


def level_of(stream_key, dims, cuts, least, top_value):
    def one(axis_at, parts):
        steps = jax.random.uniform(jax.random.fold_in(jax.random.fold_in(stream_key, 6), axis_at), (parts,), jnp.float32, least / len(cuts), top_value / len(cuts))
        return jnp.repeat(jnp.exp(steps), dims[axis_at] // parts).reshape((-1,) + (1,) * (len(dims) - axis_at - 1))

    factor_of = one(*cuts[0])
    for cut in cuts[1:]:
        factor_of = factor_of * one(*cut)
    return factor_of


def normal_values(stream_key, dims, spread, most, cuts=(), kind=jnp.bfloat16):
    values = spread * jax.random.normal(stream_key, dims, jnp.float32)
    if cuts:
        values = values * level_of(stream_key, dims, cuts, -0.22, 0.18)
    return jnp.clip(values, -most, most).astype(kind)


def setup_inputs(seed: int = 0) -> dict:
    seeds = jax.random.split(jax.random.key(seed), 8)
    queries = draw_queries(jax.random.fold_in(seeds[7], 71), 0)
    key_rows = draw_key_rows(jax.random.fold_in(seeds[7], 71), 0)
    value_rows = normal_values(seeds[2], (TOKENS, D), 1.0, 6.0, ((0, 8), (1, 4)))
    learn_rates = jnp.clip(jnp.exp(math.log(0.0025482178) - 2.3070862 * jax.random.uniform(seeds[3], (TOKENS, H), jnp.float32) ** level_of(seeds[3], (TOKENS, H), ((0, 8), (1, 4)), -0.2, 0.2)), 0.00025367737, 0.0025482178).astype(jnp.bfloat16)
    gate_fast = normal_values(seeds[4], (H, DH, DH), DH ** -0.5, 0.25, ((0, 4),), jnp.float32)
    down_fast = normal_values(seeds[5], (H, DH, DH), DH ** -0.5, 0.25, ((0, 4),), jnp.float32)
    up_fast = normal_values(seeds[6], (H, DH, DH), DH ** -0.5, 0.25, ((0, 4),), jnp.float32)
    return dict(queries=queries, key_rows=key_rows, value_rows=value_rows, learn_rates=learn_rates, gate_fast=gate_fast, down_fast=down_fast, up_fast=up_fast)


EPSILON = 1e-06

def norm_rows(values_in):
    as_float = values_in.astype(jnp.float32)
    return (as_float / jnp.sqrt(lax.optimization_barrier(jnp.mean(as_float * as_float, axis=-1, keepdims=True)) + EPSILON)).astype(jnp.bfloat16)

def fast_terms(fast_bf, key_norm, value_slice, rate_slice):
    gate_w, down_w, up_w = fast_bf
    gate_pre = jnp.dot(key_norm, gate_w, preferred_element_type=jnp.float32)
    up_pre = jnp.dot(key_norm, up_w, preferred_element_type=jnp.float32)
    sigmoid_gate = jax.nn.sigmoid(gate_pre)
    gate_act = gate_pre * sigmoid_gate
    hidden = (gate_act * up_pre).astype(jnp.bfloat16)
    scaled_val = (rate_slice.astype(jnp.float32)[:, None] * value_slice.astype(jnp.float32)).astype(jnp.bfloat16)
    hidden_grad = -jnp.dot(scaled_val, down_w.T, preferred_element_type=jnp.float32)
    gate_grad = (hidden_grad * up_pre * sigmoid_gate * (1.0 + gate_pre * (1.0 - sigmoid_gate))).astype(jnp.bfloat16)
    up_grad = (hidden_grad * gate_act).astype(jnp.bfloat16)
    gate_term = jnp.dot(key_norm.T, gate_grad, preferred_element_type=jnp.float32)
    down_term = -jnp.dot(hidden.T, scaled_val, preferred_element_type=jnp.float32)
    up_term = jnp.dot(key_norm.T, up_grad, preferred_element_type=jnp.float32)
    return (gate_term, down_term, up_term)

def rescale(weight, moved):
    target_norm = jnp.sqrt(lax.optimization_barrier(jnp.sum(weight * weight, axis=-2, keepdims=True)))
    return moved * target_norm / jnp.sqrt(lax.optimization_barrier(jnp.sum(moved * moved, axis=-2, keepdims=True)) + EPSILON)

def apply_fast(fast_bf, query_norm):
    gate_w, down_w, up_w = fast_bf
    gate_pre = jnp.dot(query_norm, gate_w, preferred_element_type=jnp.float32)
    up_pre = jnp.dot(query_norm, up_w, preferred_element_type=jnp.float32)
    hidden = (gate_pre * jax.nn.sigmoid(gate_pre) * up_pre).astype(jnp.bfloat16)
    return jnp.dot(hidden, down_w, preferred_element_type=jnp.float32).astype(jnp.bfloat16)

def by_head(matrix):
    return matrix.reshape(TOKENS, H, DH).transpose(1, 0, 2)

def one_head(inputs):
    query_slice, key_slice, value_slice, rate_slice, gate_w, down_w, up_w = inputs
    query_norm = norm_rows(query_slice)
    key_norm = norm_rows(key_slice)
    fast_f32 = (gate_w, down_w, up_w)
    pieces = []
    for group in range(2):
        lower = group * GROUP
        upper = lower + GROUP
        fast_bf = tuple((weight.astype(jnp.bfloat16) for weight in fast_f32))
        grad_terms = fast_terms(fast_bf, key_norm[lower:upper], value_slice[lower:upper], rate_slice[lower:upper])
        fast_f32 = tuple((rescale(weight, weight - summed) for weight, summed in zip(fast_f32, grad_terms)))
        renewed_bf = tuple((weight.astype(jnp.bfloat16) for weight in fast_f32))
        pieces.append(apply_fast(renewed_bf, query_norm[lower:upper]))
    return jnp.concatenate(pieces, axis=0)

def reference(queries, key_rows, value_rows, learn_rates, gate_fast, down_fast, up_fast):
    fast_heads = lax.map(one_head, (by_head(queries), by_head(key_rows), by_head(value_rows), learn_rates.T, gate_fast, down_fast, up_fast))
    fast_out = fast_heads.transpose(1, 0, 2).reshape(TOKENS, D)
    attn_heads = D // AH
    score_scale = 1.0 / math.sqrt(AH)
    pad_keys = jnp.concatenate([jnp.zeros((WINDOW, D), jnp.bfloat16), key_rows], axis=0)
    pad_values = jnp.concatenate([jnp.zeros((WINDOW, D), jnp.bfloat16), value_rows], axis=0)

    def one_block(block):
        start = block * WINDOW
        query_block = lax.dynamic_slice_in_dim(queries, start, WINDOW, 0).reshape(WINDOW, attn_heads, AH).astype(jnp.float32)
        key_block = lax.dynamic_slice_in_dim(pad_keys, start, 2 * WINDOW, 0).reshape(2 * WINDOW, attn_heads, AH).astype(jnp.float32)
        value_block = lax.dynamic_slice_in_dim(pad_values, start, 2 * WINDOW, 0).reshape(2 * WINDOW, attn_heads, AH).astype(jnp.float32)
        scores = jnp.einsum('qhd,khd->hqk', query_block, key_block) * score_scale
        query_pos = start + jnp.arange(WINDOW, dtype=jnp.int32)[:, None]
        key_pos = start - WINDOW + jnp.arange(2 * WINDOW, dtype=jnp.int32)[None, :]
        allowed = (key_pos <= query_pos) & (key_pos > query_pos - WINDOW) & (key_pos >= 0)
        scores = jnp.where(allowed[None], scores, jnp.float32(-1e+30))
        top_score = lax.optimization_barrier(jnp.max(scores, axis=-1, keepdims=True))
        expo = jnp.exp(scores - top_score)
        attend = (expo / lax.optimization_barrier(jnp.sum(expo, axis=-1, keepdims=True))).astype(jnp.bfloat16)
        return jnp.einsum('hqk,khd->qhd', attend.astype(jnp.float32), value_block).reshape(WINDOW, D)
    blocks = jnp.arange(TOKENS // WINDOW, dtype=jnp.int32)
    attended = lax.map(one_block, blocks).reshape(TOKENS, D)
    return (fast_out.astype(jnp.float32) + attended).astype(jnp.bfloat16)
```

```python
import functools
import math

import jax
import jax.numpy as jnp
from jax import lax
from jax.experimental import pallas as pl
from jax.experimental.pallas import tpu as pltpu
from jax.sharding import PartitionSpec as P

AH = 128
WINDOW = 512
TILE = 256
EPSILON = 1e-06
F32 = jnp.float32
BF16 = jnp.bfloat16


def dot(a, b, dims=((1,), (0,))):
    return lax.dot_general(a, b, (dims, ((), ())), preferred_element_type=F32)


def unit_rows(x):
    x = x.astype(F32)
    return (x * lax.rsqrt(jnp.mean(x * x, axis=-1, keepdims=True) + EPSILON)).astype(BF16)


def sigmoid(x):
    return 0.5 * jnp.tanh(0.5 * x) + 0.5


def block_of(pos_ref, d, width):
    return pl.ds(pl.multiple_of(jnp.bitwise_xor(pos_ref[0], d) * width, width), width)


def gather_weights(pos_ref, piece_refs, w_ref):
    width = piece_refs[0].shape[-1]
    for d, piece in enumerate(piece_refs):
        for m in range(3):
            w_ref[m, :, block_of(pos_ref, d, width)] = piece[m]


def grads_kernel(parts, whole, head, pos_ref, *refs):
    n_w = 3 if whole else parts
    k_ref, v_ref, r_ref = refs[:3]
    w_in = refs[3 : 3 + n_w]
    outs = refs[3 + n_w : 3 + n_w + parts]
    w_ref, acc_ref = refs[3 + n_w + parts :]
    step = pl.program_id(0)

    @pl.when(step == 0)
    def _():
        if whole:
            for m in range(3):
                w_ref[m] = w_in[m][0].astype(BF16)
        else:
            gather_weights(pos_ref, w_in, w_ref)
        acc_ref[...] = jnp.zeros_like(acc_ref)

    key_norm = unit_rows(k_ref[...])
    rate = r_ref[:, head : head + 1].astype(F32)
    scaled = (rate * v_ref[...].astype(F32)).astype(BF16)
    gate_pre = dot(key_norm, w_ref[0])
    up_pre = dot(key_norm, w_ref[1])
    grad = dot(scaled, w_ref[2], ((1,), (1,)))
    sig = sigmoid(gate_pre)
    act = gate_pre * sig
    hidden = (act * up_pre).astype(BF16)
    gate_grad = (grad * up_pre * (sig + act * (1.0 - sig))).astype(BF16)
    up_grad = (grad * act).astype(BF16)
    over_rows = ((0,), (0,))
    acc_ref[0] += dot(key_norm, gate_grad, over_rows)
    acc_ref[1] += dot(key_norm, up_grad, over_rows)
    acc_ref[2] += dot(hidden, scaled, over_rows)

    @pl.when(step == pl.num_programs(0) - 1)
    def _():
        width = outs[0].shape[-1]
        for d, out in enumerate(outs):
            for m in range(3):
                out[m] = acc_ref[m, :, block_of(pos_ref, d, width)].astype(BF16)


def grads(pos, head, parts, keys, values, rates, weights, whole, tile=512):
    rows, hw = keys.shape[0], weights[0].shape[1]
    width = hw // parts
    row_spec = pl.BlockSpec((tile, hw), lambda i, p: (i, head))
    if whole:
        w_specs = [pl.BlockSpec((1, hw, hw), lambda i, p: (head, 0, 0))] * 3
    else:
        w_specs = [pl.BlockSpec((3, hw, width), lambda i, p: (0, 0, 0))] * parts
    return pl.pallas_call(
        functools.partial(grads_kernel, parts, whole, head),
        out_shape=[jax.ShapeDtypeStruct((3, hw, width), BF16)] * parts,
        grid_spec=pltpu.PrefetchScalarGridSpec(
            num_scalar_prefetch=1,
            grid=(rows // tile,),
            in_specs=[row_spec, row_spec, pl.BlockSpec((tile, rates.shape[1]), lambda i, p: (i, 0))]
            + w_specs,
            out_specs=[pl.BlockSpec((3, hw, width), lambda i, p: (0, 0, 0))] * parts,
            scratch_shapes=[pltpu.VMEM((3, hw, hw), BF16), pltpu.VMEM((3, hw, hw), F32)],
        ),
        compiler_params=pltpu.CompilerParams(dimension_semantics=("arbitrary",)),
        cost_estimate=pl.CostEstimate(
            flops=12 * rows * hw * hw,
            bytes_accessed=4 * rows * hw + 12 * hw * hw,
            transcendentals=rows * hw,
        ),
        name="grads",
    )(pos, keys, values, rates, *weights)


def moved_shard(weight, term):
    moved = weight + term
    target = jnp.sqrt(jnp.sum(weight * weight, axis=0, keepdims=True))
    return moved * (target / jnp.sqrt(jnp.sum(moved * moved, axis=0, keepdims=True) + EPSILON))


def renew_first_kernel(pos_ref, own_ref, far_ref, g_ref, u_ref, d_ref, w_out, bf_out):
    near = pos_ref[1] == 0
    for m, w_ref in enumerate((g_ref, u_ref, d_ref)):
        term = jnp.where(near, own_ref[m].astype(F32), far_ref[m].astype(F32))
        new = moved_shard(w_ref[0], term)
        w_out[m] = new
        bf_out[m] = new.astype(BF16)


def renew_first(pos, head, own, far, gate, up, down):
    _, hw, width = own.shape
    whole = pl.BlockSpec((3, hw, width), lambda i, p: (0, 0, 0))
    shard = pl.BlockSpec((1, hw, width), lambda i, p: (head, 0, p[0]))
    return pl.pallas_call(
        renew_first_kernel,
        out_shape=[jax.ShapeDtypeStruct(own.shape, F32), jax.ShapeDtypeStruct(own.shape, BF16)],
        grid_spec=pltpu.PrefetchScalarGridSpec(
            num_scalar_prefetch=1,
            grid=(1,),
            in_specs=[whole, whole, shard, shard, shard],
            out_specs=[whole, whole],
        ),
        cost_estimate=pl.CostEstimate(flops=18 * hw * width, bytes_accessed=40 * hw * width, transcendentals=0),
        name="renew_first",
    )(pos, own, far, gate, up, down)


def renew_second_kernel(pos_ref, *refs):
    term_refs, w_ref, bf_out = refs[:-2], refs[-2], refs[-1]
    near = pos_ref[1] == 0
    for m in range(3):
        term = term_refs[0][m].astype(F32)
        for other in term_refs[1:]:
            term += other[m].astype(F32)
        weight = w_ref[m]
        bf_out[m] = jnp.where(near, weight, moved_shard(weight, term)).astype(BF16)


def renew_second(pos, terms, weight):
    _, hw, width = weight.shape
    whole = pl.BlockSpec((3, hw, width), lambda i, p: (0, 0, 0))
    return pl.pallas_call(
        renew_second_kernel,
        out_shape=jax.ShapeDtypeStruct(weight.shape, BF16),
        grid_spec=pltpu.PrefetchScalarGridSpec(
            num_scalar_prefetch=1, grid=(1,), in_specs=[whole] * (len(terms) + 1), out_specs=whole
        ),
        cost_estimate=pl.CostEstimate(flops=24 * hw * width, bytes_accessed=40 * hw * width, transcendentals=0),
        name="renew_second",
    )(pos, *terms, weight)


def attend_tile(q, keys, values, outside, half):
    scores = [dot(q, k, ((1,), (1,))) for k in keys]
    scores = [jnp.where(out, F32(-1e30), s) if out is not None else s for s, out in zip(scores, outside)]
    row = lax.broadcasted_iota(jnp.int32, (half, half), 0)
    col = lax.broadcasted_iota(jnp.int32, (half, half), 1)
    own = col <= row
    edge = jnp.where(own, scores[2], scores[0])
    top = jnp.maximum(jnp.max(edge, axis=-1, keepdims=True), jnp.max(scores[1], axis=-1, keepdims=True))
    factor = F32(math.log2(math.e) / math.sqrt(AH))
    p_edge = jnp.exp2((edge - top) * factor)
    p_mid = jnp.exp2((scores[1] - top) * factor)
    total = jnp.sum(p_edge, axis=-1, keepdims=True) + jnp.sum(p_mid, axis=-1, keepdims=True)
    zero = jnp.zeros_like(p_edge)
    probs = [jnp.where(own, zero, p_edge), p_mid, jnp.where(own, p_edge, zero)]
    out = sum(dot(p.astype(BF16), v) for p, v in zip(probs, values))
    return out * (1.0 / total)


def inner_kernel(q_ref, k_ref, v_ref, o_ref):
    half = WINDOW // 2
    for t in range(o_ref.shape[0] // half):
        keys = [k_ref[(t + j) * half : (t + j + 1) * half, :] for j in range(3)]
        values = [v_ref[(t + j) * half : (t + j + 1) * half, :] for j in range(3)]
        q = q_ref[(t + 2) * half : (t + 3) * half, :]
        o_ref[t * half : (t + 1) * half, :] = attend_tile(q, keys, values, (None, None, None), half)


def inner_attention(queries, keys, values, first, count):
    rows = queries.shape[0]
    strip = pl.BlockSpec((rows, AH), lambda a: (0, first + a))
    return pl.pallas_call(
        inner_kernel,
        out_shape=jax.ShapeDtypeStruct((rows - WINDOW, count * AH), F32),
        grid=(count,),
        in_specs=[strip] * 3,
        out_specs=pl.BlockSpec((rows - WINDOW, AH), lambda a: (0, a)),
        compiler_params=pltpu.CompilerParams(dimension_semantics=("arbitrary",)),
        cost_estimate=pl.CostEstimate(
            flops=count * rows * WINDOW * AH * 6,
            bytes_accessed=count * rows * AH * 10,
            transcendentals=count * rows * WINDOW,
        ),
        name="inner_attention",
    )(queries, keys, values)


def edge_kernel(pos_ref, q_ref, k_ref, v_ref, ha_ref, hb_ref, o_ref):
    half = WINDOW // 2
    first = pos_ref[2] == 0
    late = pos_ref[3] == 1
    halo = jnp.where(late, hb_ref[...], ha_ref[...])
    keys = [halo[0, :half], halo[0, half:], k_ref[:half, :], k_ref[half:, :]]
    values = [halo[1, :half], halo[1, half:], v_ref[:half, :], v_ref[half:, :]]
    for t in range(2):
        outside = [first if j + t < 2 else None for j in range(3)]
        o_ref[t * half : (t + 1) * half, :] = attend_tile(
            q_ref[t * half : (t + 1) * half, :], keys[t : t + 3], values[t : t + 3], outside, half
        )


def edge_attention(pos, queries, keys, values, halo_a, halo_b):
    count = queries.shape[1] // AH
    strip = pl.BlockSpec((WINDOW, AH), lambda a, p: (0, a))
    halo = pl.BlockSpec((2, WINDOW, AH), lambda a, p: (0, 0, a))
    return pl.pallas_call(
        edge_kernel,
        out_shape=jax.ShapeDtypeStruct((WINDOW, count * AH), F32),
        grid_spec=pltpu.PrefetchScalarGridSpec(
            num_scalar_prefetch=1,
            grid=(count,),
            in_specs=[strip, strip, strip, halo, halo],
            out_specs=strip,
        ),
        compiler_params=pltpu.CompilerParams(dimension_semantics=("arbitrary",)),
        cost_estimate=pl.CostEstimate(
            flops=count * WINDOW * WINDOW * AH * 6,
            bytes_accessed=count * WINDOW * AH * 18,
            transcendentals=count * WINDOW * WINDOW,
        ),
        name="edge_attention",
    )(pos, queries, keys, values, halo_a, halo_b)


def apply_kernel(parts, chained, pos_ref, *refs):
    q_ref, edge_ref, inner_ref = refs[:3]
    pieces = refs[3 : 3 + parts]
    o_ref, w_ref = refs[-2:]
    step = pl.program_id(0)

    @pl.when(step == 0)
    def _():
        gather_weights(pos_ref, pieces, w_ref)

    query_norm = unit_rows(q_ref[...])
    gate_pre = dot(query_norm, w_ref[0])
    up_pre = dot(query_norm, w_ref[1])
    hidden = (gate_pre * sigmoid(gate_pre) * up_pre).astype(BF16)
    fast = dot(hidden, w_ref[2]).astype(BF16).astype(F32)

    @pl.when(step == 0)
    def _():
        o_ref[...] = (fast + edge_ref[...]).astype(BF16)

    @pl.when(step > 0)
    def _():
        o_ref[...] = (fast + inner_ref[...]).astype(BF16)


def apply_fast(pos, head, queries, edge, inner, pieces, before):
    rows, cols = queries.shape
    parts = len(pieces)
    _, hw, width = pieces[0].shape
    in_specs = [
        pl.BlockSpec((WINDOW, hw), lambda i, p: (i, head)),
        pl.BlockSpec((WINDOW, hw), lambda i, p: (0, head)),
        pl.BlockSpec((WINDOW, hw), lambda i, p: (jnp.maximum(i - 1, 0), 0)),
    ] + [pl.BlockSpec((3, hw, width), lambda i, p: (0, 0, 0))] * parts
    operands = [pos, queries, edge, inner, *pieces]
    aliases = {}
    if before is not None:
        in_specs.append(pl.BlockSpec(memory_space=pl.ANY))
        aliases = {len(operands): 0}
        operands.append(before)
    return pl.pallas_call(
        functools.partial(apply_kernel, parts, before is not None),
        out_shape=jax.ShapeDtypeStruct((rows, cols), BF16),
        grid_spec=pltpu.PrefetchScalarGridSpec(
            num_scalar_prefetch=1,
            grid=(rows // WINDOW,),
            in_specs=in_specs,
            out_specs=pl.BlockSpec((WINDOW, hw), lambda i, p: (i, head)),
            scratch_shapes=[pltpu.VMEM((3, hw, hw), BF16)],
        ),
        input_output_aliases=aliases,
        compiler_params=pltpu.CompilerParams(dimension_semantics=("arbitrary",)),
        cost_estimate=pl.CostEstimate(
            flops=6 * rows * hw * hw, bytes_accessed=8 * rows * hw + 6 * hw * hw, transcendentals=rows * hw
        ),
        name="apply_fast",
    )(*operands)


def swap(x, d, low, high):
    return lax.ppermute(x, "seq", [(i, i ^ d) for i in range(low, high)])


def fast_device(queries, key_rows, value_rows, learn_rates, gate_fast, down_fast, up_fast):
    heads = gate_fast.shape[0]
    hw = gate_fast.shape[1]
    seq_count = lax.axis_size("seq")
    parts = seq_count // 2
    seq_index = lax.axis_index("seq").astype(jnp.int32)
    rows = queries.shape[0]
    pos = jnp.stack(
        [
            seq_index % parts,
            seq_index // parts,
            seq_index,
            (seq_index <= parts).astype(jnp.int32),
        ]
    )
    tail = jnp.stack([key_rows[rows - WINDOW :], value_rows[rows - WINDOW :]])
    early = [(i, i + 1) for i in range(parts, seq_count - 1)]
    late = [(i, i + 1) for i in range(parts)]
    halo_a = lax.ppermute(tail, "seq", early)

    first_w = (gate_fast, up_fast, down_fast)
    shards, second_terms = [], []
    w1 = []
    terms = [
        grads(pos, h, parts, key_rows, value_rows, learn_rates, first_w, True) for h in range(heads)
    ]
    per_head = hw // AH
    inner = [
        inner_attention(queries, key_rows, value_rows, h * per_head, per_head) for h in range(heads)
    ]
    far = []
    for h in range(heads):
        got = [swap(terms[h][d], d, 0, parts) for d in range(1, parts)]
        own = terms[h][0].astype(F32)
        for g in got:
            own = own + g.astype(F32)
        own = own.astype(BF16)
        far.append(lax.ppermute(own, "seq", [(i, i + parts) for i in range(parts)]))
        shard, shard_bf = renew_first(pos, h, own, far[h], *first_w)
        shards.append(shard)
        w1.append([shard_bf] + [swap(shard_bf, d, parts, seq_count) for d in range(1, parts)])
    tail_late, _ = lax.optimization_barrier((tail, far[-1]))
    halo_b = lax.ppermute(tail_late, "seq", late)
    w2 = []
    for h in range(heads):
        terms = grads(pos, h, parts, key_rows, value_rows, learn_rates, w1[h], False)
        got = [terms[0]] + [swap(terms[d], d, parts, seq_count) for d in range(1, parts)]
        shard_bf = renew_second(pos, got, shards[h])
        w2.append([shard_bf] + [swap(shard_bf, d, 0, seq_count) for d in range(1, parts)])
    edge = edge_attention(pos, queries, key_rows, value_rows, halo_a, halo_b)
    out = None
    for h in range(heads):
        out = apply_fast(pos, h, queries, edge, inner[h], w2[h], out)
    return out


def shifted(block, axis, distance):
    devices = range(lax.axis_size(axis))
    route = [(i - distance, i) for i in devices if i - distance in devices]
    return lax.ppermute(block, axis, route)


def norm_rows(values_in, heads_local, head_width):
    as_float = values_in.reshape(values_in.shape[0], heads_local, head_width).astype(jnp.float32)
    return (
        as_float / jnp.sqrt(jnp.mean(as_float * as_float, axis=-1, keepdims=True) + EPSILON)
    ).astype(jnp.bfloat16)


def fast_terms(fast_bf, key_norm, value_heads, rate_rows):
    gate_w, down_w, up_w = fast_bf
    gate_pre = jnp.einsum("nhd,hdf->nhf", key_norm, gate_w, preferred_element_type=jnp.float32)
    up_pre = jnp.einsum("nhd,hdf->nhf", key_norm, up_w, preferred_element_type=jnp.float32)
    sigmoid_gate = jax.nn.sigmoid(gate_pre)
    gate_act = gate_pre * sigmoid_gate
    hidden = (gate_act * up_pre).astype(jnp.bfloat16)
    scaled_val = (
        rate_rows.astype(jnp.float32)[:, :, None] * value_heads.astype(jnp.float32)
    ).astype(jnp.bfloat16)
    hidden_grad = -jnp.einsum(
        "nhe,hfe->nhf", scaled_val, down_w, preferred_element_type=jnp.float32
    )
    gate_grad = (
        hidden_grad * up_pre * sigmoid_gate * (1.0 + gate_pre * (1.0 - sigmoid_gate))
    ).astype(jnp.bfloat16)
    up_grad = (hidden_grad * gate_act).astype(jnp.bfloat16)
    gate_term = jnp.einsum("nhd,nhf->hdf", key_norm, gate_grad, preferred_element_type=jnp.float32)
    down_term = -jnp.einsum("nhf,nhe->hfe", hidden, scaled_val, preferred_element_type=jnp.float32)
    up_term = jnp.einsum("nhd,nhf->hdf", key_norm, up_grad, preferred_element_type=jnp.float32)
    return (gate_term, down_term, up_term)


def rescale(weight, moved):
    target_norm = jnp.sqrt(jnp.sum(weight * weight, axis=-2, keepdims=True))
    return moved * target_norm / jnp.sqrt(jnp.sum(moved * moved, axis=-2, keepdims=True) + EPSILON)


def general_apply(fast_bf, query_norm):
    gate_w, down_w, up_w = fast_bf
    gate_pre = jnp.einsum("nhd,hdf->nhf", query_norm, gate_w, preferred_element_type=jnp.float32)
    up_pre = jnp.einsum("nhd,hdf->nhf", query_norm, up_w, preferred_element_type=jnp.float32)
    hidden = (gate_pre * jax.nn.sigmoid(gate_pre) * up_pre).astype(jnp.bfloat16)
    return jnp.einsum("nhf,hfe->nhe", hidden, down_w, preferred_element_type=jnp.float32).astype(
        jnp.bfloat16
    )


def renew(fast_f32, grad_terms):
    grad_sums = lax.psum((grad_terms[0], grad_terms[1], grad_terms[2]), "seq")
    renewed = tuple(
        (rescale(weight, weight - summed) for weight, summed in zip(fast_f32, grad_sums))
    )
    renewed_bf = tuple((weight.astype(jnp.bfloat16) for weight in renewed))
    return (renewed, renewed_bf)


def general_device(queries, key_rows, value_rows, learn_rates, gate_fast, down_fast, up_fast):
    heads_local = gate_fast.shape[0]
    head_width = gate_fast.shape[1]
    seq_count = lax.axis_size("seq")
    seq_index = lax.axis_index("seq")
    rows_here = queries.shape[0]
    width_here = queries.shape[1]
    fast_f32 = (gate_fast, down_fast, up_fast)
    first_bf = tuple((weight.astype(jnp.bfloat16) for weight in fast_f32))
    own_group = (seq_index >= seq_count // 2).astype(jnp.int32)
    query_norm = norm_rows(queries, heads_local, head_width)
    key_norm = norm_rows(key_rows, heads_local, head_width)
    value_heads = value_rows.reshape(rows_here, heads_local, head_width)
    fast_bf = first_bf
    kept = []
    for group in range(2):
        group_rates = jnp.where(own_group == group, learn_rates, jnp.zeros_like(learn_rates))
        grad_terms = fast_terms(fast_bf, key_norm, value_heads, group_rates)
        fast_f32, fast_bf = renew(fast_f32, grad_terms)
        kept.append(fast_bf)
    chosen = tuple(
        (jnp.where(own_group == 0, early, later) for early, later in zip(kept[0], kept[1]))
    )
    fast_out = general_apply(chosen, query_norm).reshape(rows_here, width_here)
    attn_heads = width_here // AH
    score_scale = 1.0 / math.sqrt(AH)
    prev_keys, prev_values = shifted(
        (key_rows[rows_here - WINDOW :], value_rows[rows_here - WINDOW :]), "seq", 1
    )
    wide_keys = jnp.concatenate([prev_keys, key_rows], axis=0)
    wide_values = jnp.concatenate([prev_values, value_rows], axis=0)
    query_offset = jnp.arange(WINDOW, dtype=jnp.int32)[:, None]
    key_offset = jnp.arange(2 * WINDOW, dtype=jnp.int32)[None, :]
    block_outs = []
    for block in range(rows_here // WINDOW):
        lower = block * WINDOW
        start = seq_index * rows_here + lower
        query_block = queries[lower : lower + WINDOW].reshape(WINDOW, attn_heads, AH)
        key_block = wide_keys[lower : lower + 2 * WINDOW].reshape(2 * WINDOW, attn_heads, AH)
        value_block = wide_values[lower : lower + 2 * WINDOW].reshape(2 * WINDOW, attn_heads, AH)
        scores = (
            jnp.einsum("qhd,khd->hqk", query_block, key_block, preferred_element_type=jnp.float32)
            * score_scale
        )
        query_pos = start + query_offset
        key_pos = start - WINDOW + key_offset
        allowed = (key_pos <= query_pos) & (key_pos > query_pos - WINDOW) & (key_pos >= 0)
        scores = jnp.where(allowed[None], scores, jnp.float32(-1e30))
        top_score = jnp.max(scores, axis=-1, keepdims=True)
        expo = jnp.exp(scores - top_score)
        attend = (expo / jnp.sum(expo, axis=-1, keepdims=True)).astype(jnp.bfloat16)
        block_outs.append(
            jnp.einsum(
                "hqk,khd->qhd", attend, value_block, preferred_element_type=jnp.float32
            ).reshape(WINDOW, width_here)
        )
    attended = jnp.concatenate(block_outs, axis=0)
    return (fast_out.astype(jnp.float32) + attended).astype(jnp.bfloat16)


def solution(mesh):
    parts = mesh.shape["seq"] // 2

    def on_device(*args):
        width = args[4].shape[1] // parts
        if parts & (parts - 1) == 0 and width % AH == 0 and args[0].shape[0] >= 2 * WINDOW:
            return fast_device(*args)
        return general_device(*args)

    return jax.shard_map(
        on_device,
        mesh=mesh,
        in_specs=(
            P("seq", "head"),
            P("seq", "head"),
            P("seq", "head"),
            P("seq", "head"),
            P("head", None, None),
            P("head", None, None),
            P("head", None, None),
        ),
        out_specs=P("seq", "head"),
        check_vma=False,
    )
```

```python
import functools
import math

import jax
import jax.numpy as jnp
from jax import lax
from jax.experimental import pallas as pl
from jax.experimental.pallas import tpu as pltpu
from jax.sharding import PartitionSpec as P


AH = 128
WINDOW = 512
EPSILON = 1e-06
F32 = jnp.float32
BF16 = jnp.bfloat16


def dot(a, b, dims=((1,), (0,))):
    return lax.dot_general(a, b, (dims, ((), ())), preferred_element_type=F32)


def unit_rows(x):
    x = x.astype(F32)
    return (x * lax.rsqrt(jnp.mean(x * x, axis=-1, keepdims=True) + EPSILON)).astype(BF16)


def sigmoid(x):
    return 0.5 * jnp.tanh(0.5 * x) + 0.5


def block_of(pos_ref, d, width):
    return pl.ds(pl.multiple_of(jnp.bitwise_xor(pos_ref[0], d) * width, width), width)


def gather_weights(pos_ref, piece_refs, w_ref):
    width = piece_refs[0].shape[-1]
    for d, piece in enumerate(piece_refs):
        for m in range(3):
            w_ref[m, :, block_of(pos_ref, d, width)] = piece[m]


def grads_kernel(parts, whole, head, pos_ref, *refs):
    n_w = 3 if whole else parts
    k_ref, v_ref, r_ref = refs[:3]
    w_in = refs[3 : 3 + n_w]
    outs = refs[3 + n_w : 3 + n_w + parts]
    w_ref, acc_ref = refs[-2:]
    step = pl.program_id(0)

    @pl.when(step == 0)
    def _():
        if whole:
            for m in range(3):
                w_ref[m] = w_in[m][0].astype(BF16)
        else:
            gather_weights(pos_ref, w_in, w_ref)
        acc_ref[...] = jnp.zeros_like(acc_ref)

    key_norm = unit_rows(k_ref[...])
    rate = jnp.transpose(jnp.broadcast_to(r_ref[head : head + 1, :].astype(F32), (8, r_ref.shape[1])))[:, :1]
    scaled = (rate * v_ref[...].astype(F32)).astype(BF16)
    gate_pre = dot(key_norm, w_ref[0])
    up_pre = dot(key_norm, w_ref[1])
    grad = dot(scaled, w_ref[2], ((1,), (1,)))
    sig = sigmoid(gate_pre)
    act = gate_pre * sig
    hidden = (act * up_pre).astype(BF16)
    gate_grad = (grad * up_pre * (sig + act * (1.0 - sig))).astype(BF16)
    up_grad = (grad * act).astype(BF16)
    over_rows = ((0,), (0,))
    acc_ref[0] += dot(key_norm, gate_grad, over_rows)
    acc_ref[1] += dot(key_norm, up_grad, over_rows)
    acc_ref[2] += dot(hidden, scaled, over_rows)

    @pl.when(step == pl.num_programs(0) - 1)
    def _():
        width = outs[0].shape[-1]
        for d, out in enumerate(outs):
            for m in range(3):
                out[m] = acc_ref[m, :, block_of(pos_ref, d, width)].astype(BF16)


def grads(pos, head, parts, keys, values, rates, weights, whole, tile=WINDOW):
    rows, hw = keys.shape[0], weights[0].shape[1]
    width = hw // parts
    row_spec = pl.BlockSpec((tile, hw), lambda i, p: (i, head))
    if whole:
        w_specs = [pl.BlockSpec((1, hw, hw), lambda i, p: (head, 0, 0))] * 3
    else:
        w_specs = [pl.BlockSpec((3, hw, width), lambda i, p: (0, 0, 0))] * parts
    return pl.pallas_call(
        functools.partial(grads_kernel, parts, whole, head),
        out_shape=[jax.ShapeDtypeStruct((3, hw, width), BF16)] * parts,
        grid_spec=pltpu.PrefetchScalarGridSpec(
            num_scalar_prefetch=1,
            grid=(rows // tile,),
            in_specs=[row_spec, row_spec, pl.BlockSpec((rates.shape[0], tile), lambda i, p: (0, i))]
            + w_specs,
            out_specs=[pl.BlockSpec((3, hw, width), lambda i, p: (0, 0, 0))] * parts,
            scratch_shapes=[pltpu.VMEM((3, hw, hw), BF16), pltpu.VMEM((3, hw, hw), F32)],
        ),
        compiler_params=pltpu.CompilerParams(dimension_semantics=("arbitrary",)),
        cost_estimate=pl.CostEstimate(
            flops=12 * rows * hw * hw,
            bytes_accessed=4 * rows * hw + 12 * hw * hw,
            transcendentals=rows * hw,
        ),
        name="grads",
    )(pos, keys, values, rates, *weights)


def tail_kernel(k_ref, v_ref, o_ref):
    o_ref[0] = k_ref[...]
    o_ref[1] = v_ref[...]


def tail_rows(keys, values, step=256):
    rows, cols = keys.shape
    first = (rows - WINDOW) // step
    spec = pl.BlockSpec((step, cols), lambda i: (first + i, 0))
    return pl.pallas_call(
        tail_kernel,
        out_shape=jax.ShapeDtypeStruct((2, WINDOW, cols), BF16),
        grid=(WINDOW // step,),
        in_specs=[spec, spec],
        out_specs=pl.BlockSpec((2, step, cols), lambda i: (0, i, 0)),
        compiler_params=pltpu.CompilerParams(dimension_semantics=("arbitrary",)),
        cost_estimate=pl.CostEstimate(flops=0, bytes_accessed=8 * WINDOW * cols, transcendentals=0),
        name="tail_rows",
    )(keys, values)


def moved_shard(weight, term):
    moved = weight + term
    target = jnp.sqrt(jnp.sum(weight * weight, axis=0, keepdims=True))
    return moved * (target / jnp.sqrt(jnp.sum(moved * moved, axis=0, keepdims=True) + EPSILON))


def renew_first_kernel(pos_ref, own_ref, far_ref, g_ref, u_ref, d_ref, w_out, bf_out):
    near = pos_ref[1] == 0
    for m, w_ref in enumerate((g_ref, u_ref, d_ref)):
        term = jnp.where(near, own_ref[m].astype(F32), far_ref[m].astype(F32))
        new = moved_shard(w_ref[0], term)
        w_out[m] = new
        bf_out[m] = new.astype(BF16)


def renew_first(pos, head, own, far, gate, up, down):
    _, hw, width = own.shape
    whole = pl.BlockSpec((3, hw, width), lambda i, p: (0, 0, 0))
    shard = pl.BlockSpec((1, hw, width), lambda i, p: (head, 0, p[0]))
    return pl.pallas_call(
        renew_first_kernel,
        out_shape=[jax.ShapeDtypeStruct(own.shape, F32), jax.ShapeDtypeStruct(own.shape, BF16)],
        grid_spec=pltpu.PrefetchScalarGridSpec(
            num_scalar_prefetch=1,
            grid=(1,),
            in_specs=[whole, whole, shard, shard, shard],
            out_specs=[whole, whole],
        ),
        cost_estimate=pl.CostEstimate(flops=18 * hw * width, bytes_accessed=40 * hw * width, transcendentals=0),
        name="renew_first",
    )(pos, own, far, gate, up, down)


def renew_second_kernel(pos_ref, *refs):
    term_refs, w_ref, bf_out = refs[:-2], refs[-2], refs[-1]
    near = pos_ref[1] == 0
    for m in range(3):
        term = term_refs[0][m].astype(F32)
        for other in term_refs[1:]:
            term += other[m].astype(F32)
        weight = w_ref[m]
        bf_out[m] = jnp.where(near, weight, moved_shard(weight, term)).astype(BF16)


def renew_second(pos, terms, weight):
    _, hw, width = weight.shape
    whole = pl.BlockSpec((3, hw, width), lambda i, p: (0, 0, 0))
    return pl.pallas_call(
        renew_second_kernel,
        out_shape=jax.ShapeDtypeStruct(weight.shape, BF16),
        grid_spec=pltpu.PrefetchScalarGridSpec(
            num_scalar_prefetch=1, grid=(1,), in_specs=[whole] * (len(terms) + 1), out_specs=whole
        ),
        cost_estimate=pl.CostEstimate(flops=24 * hw * width, bytes_accessed=40 * hw * width, transcendentals=0),
        name="renew_second",
    )(pos, *terms, weight)


def attend_tile(q, keys, values, outside, half):
    scores = [dot(q, k, ((1,), (1,))) for k in keys]
    scores = [jnp.where(out, F32(-1e30), s) if out is not None else s for s, out in zip(scores, outside)]
    row = lax.broadcasted_iota(jnp.int32, (half, half), 0)
    col = lax.broadcasted_iota(jnp.int32, (half, half), 1)
    own = col <= row
    edge = jnp.where(own, scores[2], scores[0])
    top = jnp.maximum(jnp.max(edge, axis=-1, keepdims=True), jnp.max(scores[1], axis=-1, keepdims=True))
    factor = F32(math.log2(math.e) / math.sqrt(AH))
    p_edge = jnp.exp2((edge - top) * factor)
    p_mid = jnp.exp2((scores[1] - top) * factor)
    total = jnp.sum(p_edge, axis=-1, keepdims=True) + jnp.sum(p_mid, axis=-1, keepdims=True)
    zero = jnp.zeros_like(p_edge)
    probs = [jnp.where(own, zero, p_edge), p_mid, jnp.where(own, p_edge, zero)]
    out = sum(dot(p.astype(BF16), v) for p, v in zip(probs, values))
    return (out * (1.0 / total)).astype(BF16)


def inner_kernel(q_ref, k_ref, v_ref, _, o_ref):
    half = WINDOW // 2
    for t in range(o_ref.shape[0] // half):
        keys = [k_ref[(t + j) * half : (t + j + 1) * half, :] for j in range(3)]
        values = [v_ref[(t + j) * half : (t + j + 1) * half, :] for j in range(3)]
        q = q_ref[(t + 2) * half : (t + 3) * half, :]
        o_ref[t * half : (t + 1) * half, :] = attend_tile(q, keys, values, (None, None, None), half)


def inner_attention(queries, keys, values, first, count, after):
    rows = queries.shape[0]
    strip = pl.BlockSpec((rows, AH), lambda a: (0, first + a))
    return pl.pallas_call(
        inner_kernel,
        out_shape=jax.ShapeDtypeStruct((rows - WINDOW, count * AH), BF16),
        grid=(count,),
        in_specs=[strip] * 3 + [pl.BlockSpec(memory_space=pl.ANY)],
        out_specs=pl.BlockSpec((rows - WINDOW, AH), lambda a: (0, a)),
        compiler_params=pltpu.CompilerParams(dimension_semantics=("arbitrary",)),
        cost_estimate=pl.CostEstimate(
            flops=count * rows * WINDOW * AH * 6,
            bytes_accessed=count * rows * AH * 10,
            transcendentals=count * rows * WINDOW,
        ),
        name="inner_attention",
    )(queries, keys, values, after)


def edge_kernel(side, pos_ref, q_ref, k_ref, v_ref, h_ref, *refs):
    o_ref = refs[-1]
    half = WINDOW // 2
    active = pos_ref[1] == side

    @pl.when(active)
    def _():
        first = pos_ref[2] == 0
        keys = [h_ref[0, :half], h_ref[0, half:], k_ref[:half, :], k_ref[half:, :]]
        values = [h_ref[1, :half], h_ref[1, half:], v_ref[:half, :], v_ref[half:, :]]
        for t in range(2):
            outside = [first if j + t < 2 else None for j in range(3)]
            o_ref[t * half : (t + 1) * half, :] = attend_tile(
                q_ref[t * half : (t + 1) * half, :], keys[t : t + 3], values[t : t + 3], outside, half
            )

    @pl.when(jnp.logical_not(active))
    def _():
        o_ref[...] = refs[0][...] if len(refs) > 1 else jnp.zeros_like(o_ref)


def edge_attention(pos, queries, keys, values, halo, before, side):
    count = queries.shape[1] // AH
    strip = pl.BlockSpec((WINDOW, AH), lambda a, p: (0, jnp.where(p[1] == side, a, 0)))
    return pl.pallas_call(
        functools.partial(edge_kernel, side),
        out_shape=jax.ShapeDtypeStruct((WINDOW, count * AH), BF16),
        grid_spec=pltpu.PrefetchScalarGridSpec(
            num_scalar_prefetch=1,
            grid=(count,),
            in_specs=[strip, strip, strip]
            + [pl.BlockSpec((2, WINDOW, AH), lambda a, p: (0, 0, jnp.where(p[1] == side, a, 0)))]
            + [pl.BlockSpec((WINDOW, AH), lambda a, p: (0, 0))] * len(before),
            out_specs=strip,
        ),
        input_output_aliases={5: 0} if before else {},
        compiler_params=pltpu.CompilerParams(dimension_semantics=("arbitrary",)),
        cost_estimate=pl.CostEstimate(
            flops=count * WINDOW * WINDOW * AH * 6,
            bytes_accessed=count * WINDOW * AH * 18,
            transcendentals=count * WINDOW * WINDOW,
        ),
        name="edge_attention",
    )(pos, queries, keys, values, halo, *before)


def apply_kernel(parts, pos_ref, *refs):
    q_ref, edge_ref, inner_ref = refs[:3]
    pieces = refs[3 : 3 + parts]
    o_ref, w_ref = refs[-2:]
    step = pl.program_id(0)

    @pl.when(step == 0)
    def _():
        gather_weights(pos_ref, pieces, w_ref)

    query_norm = unit_rows(q_ref[...])
    gate_pre = dot(query_norm, w_ref[0])
    up_pre = dot(query_norm, w_ref[1])
    hidden = (gate_pre * sigmoid(gate_pre) * up_pre).astype(BF16)
    fast = dot(hidden, w_ref[2]).astype(BF16).astype(F32)

    @pl.when(step == 0)
    def _():
        o_ref[...] = (fast + edge_ref[...].astype(F32)).astype(BF16)

    @pl.when(step > 0)
    def _():
        o_ref[...] = (fast + inner_ref[...].astype(F32)).astype(BF16)


def apply_fast(pos, head, queries, edge, inner, pieces, before):
    rows, cols = queries.shape
    parts = len(pieces)
    _, hw, width = pieces[0].shape
    in_specs = [
        pl.BlockSpec((WINDOW, hw), lambda i, p: (i, head)),
        pl.BlockSpec((WINDOW, hw), lambda i, p: (0, head)),
        pl.BlockSpec((WINDOW, hw), lambda i, p: (jnp.maximum(i - 1, 0), 0)),
    ] + [pl.BlockSpec((3, hw, width), lambda i, p: (0, 0, 0))] * parts
    operands = [pos, queries, edge, inner, *pieces]
    aliases = {}
    if before is not None:
        in_specs.append(pl.BlockSpec(memory_space=pl.ANY))
        aliases = {len(operands): 0}
        operands.append(before)
    return pl.pallas_call(
        functools.partial(apply_kernel, parts),
        out_shape=jax.ShapeDtypeStruct((rows, cols), BF16),
        grid_spec=pltpu.PrefetchScalarGridSpec(
            num_scalar_prefetch=1,
            grid=(rows // WINDOW,),
            in_specs=in_specs,
            out_specs=pl.BlockSpec((WINDOW, hw), lambda i, p: (i, head)),
            scratch_shapes=[pltpu.VMEM((3, hw, hw), BF16)],
        ),
        input_output_aliases=aliases,
        compiler_params=pltpu.CompilerParams(dimension_semantics=("arbitrary",)),
        cost_estimate=pl.CostEstimate(
            flops=6 * rows * hw * hw, bytes_accessed=8 * rows * hw + 6 * hw * hw, transcendentals=rows * hw
        ),
        name="apply_fast",
    )(*operands)


def hop(x, route):
    return lax.ppermute(x, "seq", route)


def spread(xs, low, high):
    return [hop(x, [(i, i ^ d) for i in range(low, high)]) for d, x in enumerate(xs) if d]


def fast_device(queries, key_rows, value_rows, learn_rates, gate_fast, down_fast, up_fast):
    heads, hw = gate_fast.shape[:2]
    seq_count = lax.axis_size("seq")
    parts = seq_count // 2
    seq_index = lax.axis_index("seq").astype(jnp.int32)
    pos = jnp.stack([seq_index % parts, seq_index // parts, seq_index])
    early = [(i, i + 1) for i in range(parts - 1, seq_count - 1)]
    late = [(i, i + 1) for i in range(parts - 1)]
    across = [(i, i + parts) for i in range(parts)]
    per_head = hw // AH
    rates = learn_rates.T
    first_w = (gate_fast, up_fast, down_fast)
    span = range(heads)

    tail = tail_rows(key_rows, value_rows)
    halo_a = hop(tail, early)
    terms = [grads(pos, h, parts, key_rows, value_rows, rates, first_w, True) for h in span]
    shards, w1, far, inner = [], [], [], []
    for h in span:
        got = spread(terms[h], 0, parts)
        own = terms[h][0].astype(F32)
        for g in got:
            own = own + g.astype(F32)
        own = own.astype(BF16)
        far.append(hop(own, across))
        inner.append(inner_attention(queries, key_rows, value_rows, h * per_head, per_head, own))
        shard, shard_bf = renew_first(pos, h, own, far[h], *first_w)
        shards.append(shard)
        w1.append([shard_bf] + spread([shard_bf] * parts, parts, seq_count))
    edge = edge_attention(pos, queries, key_rows, value_rows, halo_a, (), 1)
    tail, _ = lax.optimization_barrier((tail, far[-1]))
    halo_b = hop(tail, late)
    w2 = []
    for h in span:
        term = grads(pos, h, parts, key_rows, value_rows, rates, w1[h], False)
        got = [term[0]] + spread(term, parts, seq_count)
        shard_bf = renew_second(pos, got, shards[h])
        w2.append([shard_bf] + spread([shard_bf] * parts, 0, seq_count))
    edge = edge_attention(pos, queries, key_rows, value_rows, halo_b, (edge,), 0)
    out = None
    for h in span:
        out = apply_fast(pos, h, queries, edge, inner[h], w2[h], out)
    return out


def shifted(block, axis, distance):
    devices = range(lax.axis_size(axis))
    route = [(i - distance, i) for i in devices if i - distance in devices]
    return lax.ppermute(block, axis, route)


def norm_rows(values_in, heads_local, head_width):
    as_float = values_in.reshape(values_in.shape[0], heads_local, head_width).astype(jnp.float32)
    return (
        as_float / jnp.sqrt(jnp.mean(as_float * as_float, axis=-1, keepdims=True) + EPSILON)
    ).astype(jnp.bfloat16)


def fast_terms(fast_bf, key_norm, value_heads, rate_rows):
    gate_w, down_w, up_w = fast_bf
    gate_pre = jnp.einsum("nhd,hdf->nhf", key_norm, gate_w, preferred_element_type=jnp.float32)
    up_pre = jnp.einsum("nhd,hdf->nhf", key_norm, up_w, preferred_element_type=jnp.float32)
    sigmoid_gate = jax.nn.sigmoid(gate_pre)
    gate_act = gate_pre * sigmoid_gate
    hidden = (gate_act * up_pre).astype(jnp.bfloat16)
    scaled_val = (
        rate_rows.astype(jnp.float32)[:, :, None] * value_heads.astype(jnp.float32)
    ).astype(jnp.bfloat16)
    hidden_grad = -jnp.einsum(
        "nhe,hfe->nhf", scaled_val, down_w, preferred_element_type=jnp.float32
    )
    gate_grad = (
        hidden_grad * up_pre * sigmoid_gate * (1.0 + gate_pre * (1.0 - sigmoid_gate))
    ).astype(jnp.bfloat16)
    up_grad = (hidden_grad * gate_act).astype(jnp.bfloat16)
    gate_term = jnp.einsum("nhd,nhf->hdf", key_norm, gate_grad, preferred_element_type=jnp.float32)
    down_term = -jnp.einsum("nhf,nhe->hfe", hidden, scaled_val, preferred_element_type=jnp.float32)
    up_term = jnp.einsum("nhd,nhf->hdf", key_norm, up_grad, preferred_element_type=jnp.float32)
    return (gate_term, down_term, up_term)


def rescale(weight, moved):
    target_norm = jnp.sqrt(jnp.sum(weight * weight, axis=-2, keepdims=True))
    return moved * target_norm / jnp.sqrt(jnp.sum(moved * moved, axis=-2, keepdims=True) + EPSILON)


def general_apply(fast_bf, query_norm):
    gate_w, down_w, up_w = fast_bf
    gate_pre = jnp.einsum("nhd,hdf->nhf", query_norm, gate_w, preferred_element_type=jnp.float32)
    up_pre = jnp.einsum("nhd,hdf->nhf", query_norm, up_w, preferred_element_type=jnp.float32)
    hidden = (gate_pre * jax.nn.sigmoid(gate_pre) * up_pre).astype(jnp.bfloat16)
    return jnp.einsum("nhf,hfe->nhe", hidden, down_w, preferred_element_type=jnp.float32).astype(
        jnp.bfloat16
    )


def renew(fast_f32, grad_terms):
    grad_sums = lax.psum((grad_terms[0], grad_terms[1], grad_terms[2]), "seq")
    renewed = tuple(
        (rescale(weight, weight - summed) for weight, summed in zip(fast_f32, grad_sums))
    )
    renewed_bf = tuple((weight.astype(jnp.bfloat16) for weight in renewed))
    return (renewed, renewed_bf)


def general_device(queries, key_rows, value_rows, learn_rates, gate_fast, down_fast, up_fast):
    heads_local = gate_fast.shape[0]
    head_width = gate_fast.shape[1]
    seq_count = lax.axis_size("seq")
    seq_index = lax.axis_index("seq")
    rows_here = queries.shape[0]
    width_here = queries.shape[1]
    fast_f32 = (gate_fast, down_fast, up_fast)
    first_bf = tuple((weight.astype(jnp.bfloat16) for weight in fast_f32))
    own_group = (seq_index >= seq_count // 2).astype(jnp.int32)
    query_norm = norm_rows(queries, heads_local, head_width)
    key_norm = norm_rows(key_rows, heads_local, head_width)
    value_heads = value_rows.reshape(rows_here, heads_local, head_width)
    fast_bf = first_bf
    kept = []
    for group in range(2):
        group_rates = jnp.where(own_group == group, learn_rates, jnp.zeros_like(learn_rates))
        grad_terms = fast_terms(fast_bf, key_norm, value_heads, group_rates)
        fast_f32, fast_bf = renew(fast_f32, grad_terms)
        kept.append(fast_bf)
    chosen = tuple(
        (jnp.where(own_group == 0, early, later) for early, later in zip(kept[0], kept[1]))
    )
    fast_out = general_apply(chosen, query_norm).reshape(rows_here, width_here)
    attn_heads = width_here // AH
    score_scale = 1.0 / math.sqrt(AH)
    prev_keys, prev_values = shifted(
        (key_rows[rows_here - WINDOW :], value_rows[rows_here - WINDOW :]), "seq", 1
    )
    wide_keys = jnp.concatenate([prev_keys, key_rows], axis=0)
    wide_values = jnp.concatenate([prev_values, value_rows], axis=0)
    query_offset = jnp.arange(WINDOW, dtype=jnp.int32)[:, None]
    key_offset = jnp.arange(2 * WINDOW, dtype=jnp.int32)[None, :]
    block_outs = []
    for block in range(rows_here // WINDOW):
        lower = block * WINDOW
        start = seq_index * rows_here + lower
        query_block = queries[lower : lower + WINDOW].reshape(WINDOW, attn_heads, AH)
        key_block = wide_keys[lower : lower + 2 * WINDOW].reshape(2 * WINDOW, attn_heads, AH)
        value_block = wide_values[lower : lower + 2 * WINDOW].reshape(2 * WINDOW, attn_heads, AH)
        scores = (
            jnp.einsum("qhd,khd->hqk", query_block, key_block, preferred_element_type=jnp.float32)
            * score_scale
        )
        query_pos = start + query_offset
        key_pos = start - WINDOW + key_offset
        allowed = (key_pos <= query_pos) & (key_pos > query_pos - WINDOW) & (key_pos >= 0)
        scores = jnp.where(allowed[None], scores, jnp.float32(-1e30))
        top_score = jnp.max(scores, axis=-1, keepdims=True)
        expo = jnp.exp(scores - top_score)
        attend = (expo / jnp.sum(expo, axis=-1, keepdims=True)).astype(jnp.bfloat16)
        block_outs.append(
            jnp.einsum(
                "hqk,khd->qhd", attend, value_block, preferred_element_type=jnp.float32
            ).reshape(WINDOW, width_here)
        )
    attended = jnp.concatenate(block_outs, axis=0)
    return (fast_out.astype(jnp.float32) + attended).astype(jnp.bfloat16)


def solution(mesh):
    parts = mesh.shape["seq"] // 2

    def fits(args):
        width = args[4].shape[1] // parts
        return parts & (parts - 1) == 0 and width % AH == 0 and args[0].shape[0] >= 2 * WINDOW

    def on_device(*args):
        if fits(args):
            return fast_device(*args)
        return general_device(*args)

    return jax.shard_map(
        on_device,
        mesh=mesh,
        in_specs=(
            P("seq", "head"),
            P("seq", "head"),
            P("seq", "head"),
            P("seq", "head"),
            P("head", None, None),
            P("head", None, None),
            P("head", None, None),
        ),
        out_specs=P("seq", "head"),
        check_vma=False,
    )
```

```python
import functools
import math

import jax
import jax.numpy as jnp
from jax import lax
from jax.experimental import pallas as pl
from jax.experimental.pallas import tpu as pltpu
from jax.sharding import PartitionSpec as P


AH = 128
WINDOW = 512
EPSILON = 1e-06
GRANT = 28 * 2**20
F32 = jnp.float32
BF16 = jnp.bfloat16


def dot(a, b, dims=((1,), (0,))):
    return lax.dot_general(a, b, (dims, ((), ())), preferred_element_type=F32)


def unit_rows(x):
    x = x.astype(F32)
    return (x * lax.rsqrt(jnp.mean(x * x, axis=-1, keepdims=True) + EPSILON)).astype(BF16)


def sigmoid(x):
    return 0.5 * jnp.tanh(0.5 * x) + 0.5


def block_of(pos_ref, d, width):
    return pl.ds(pl.multiple_of(jnp.bitwise_xor(pos_ref[0], d) * width, width), width)


def gather_weights(pos_ref, piece_refs, w_ref):
    width = piece_refs[0].shape[-1]
    for d, piece in enumerate(piece_refs):
        for m in range(3):
            w_ref[m, :, block_of(pos_ref, d, width)] = piece[m]


def grads_kernel(parts, whole, head, pos_ref, *refs):
    n_w = 3 if whole else parts
    k_ref, v_ref, r_ref = refs[:3]
    w_in = refs[3 : 3 + n_w]
    outs = refs[3 + n_w : 3 + n_w + parts]
    w_ref, acc_ref = refs[-2:]
    step = pl.program_id(0)

    @pl.when(step == 0)
    def _():
        if whole:
            for m in range(3):
                w_ref[m] = w_in[m][0].astype(BF16)
        else:
            gather_weights(pos_ref, w_in, w_ref)
        acc_ref[...] = jnp.zeros_like(acc_ref)

    key_norm = unit_rows(k_ref[...])
    rate = jnp.transpose(jnp.broadcast_to(r_ref[head : head + 1, :].astype(F32), (8, r_ref.shape[1])))[:, :1]
    scaled = (rate * v_ref[...].astype(F32)).astype(BF16)
    gate_pre = dot(key_norm, w_ref[0])
    up_pre = dot(key_norm, w_ref[1])
    grad = dot(scaled, w_ref[2], ((1,), (1,)))
    sig = sigmoid(gate_pre)
    act = gate_pre * sig
    hidden = (act * up_pre).astype(BF16)
    gate_grad = (grad * up_pre * (sig + act * (1.0 - sig))).astype(BF16)
    up_grad = (grad * act).astype(BF16)
    over_rows = ((0,), (0,))
    acc_ref[0] += dot(key_norm, gate_grad, over_rows)
    acc_ref[1] += dot(key_norm, up_grad, over_rows)
    acc_ref[2] += dot(hidden, scaled, over_rows)

    @pl.when(step == pl.num_programs(0) - 1)
    def _():
        width = outs[0].shape[-1]
        for d, out in enumerate(outs):
            for m in range(3):
                out[m] = acc_ref[m, :, block_of(pos_ref, d, width)].astype(BF16)


def grads(pos, head, parts, keys, values, rates, weights, whole, tile=WINDOW):
    rows, hw = keys.shape[0], weights[0].shape[1]
    width = hw // parts
    row_spec = pl.BlockSpec((tile, hw), lambda i, p: (i, head))
    if whole:
        w_specs = [pl.BlockSpec((1, hw, hw), lambda i, p: (head, 0, 0))] * 3
    else:
        w_specs = [pl.BlockSpec((3, hw, width), lambda i, p: (0, 0, 0))] * parts
    return pl.pallas_call(
        functools.partial(grads_kernel, parts, whole, head),
        out_shape=[jax.ShapeDtypeStruct((3, hw, width), BF16)] * parts,
        grid_spec=pltpu.PrefetchScalarGridSpec(
            num_scalar_prefetch=1,
            grid=(rows // tile,),
            in_specs=[row_spec, row_spec, pl.BlockSpec((rates.shape[0], tile), lambda i, p: (0, i))]
            + w_specs,
            out_specs=[pl.BlockSpec((3, hw, width), lambda i, p: (0, 0, 0))] * parts,
            scratch_shapes=[pltpu.VMEM((3, hw, hw), BF16), pltpu.VMEM((3, hw, hw), F32)],
        ),
        compiler_params=pltpu.CompilerParams(dimension_semantics=("arbitrary",)),
        cost_estimate=pl.CostEstimate(
            flops=12 * rows * hw * hw,
            bytes_accessed=4 * rows * hw + 12 * hw * hw,
            transcendentals=rows * hw,
        ),
    )(pos, keys, values, rates, *weights)


def tail_kernel(k_ref, v_ref, main_ref, rest_ref):
    cut = main_ref.shape[-1]
    for m, ref in enumerate((k_ref, v_ref)):
        main_ref[m] = ref[:, :cut]
        rest_ref[m] = ref[:, cut:]


def tail_rows(keys, values, kept, step=256):
    rows, cols = keys.shape
    first = (rows - WINDOW) // step
    spec = pl.BlockSpec((step, cols), lambda i: (first + i, 0))
    return pl.pallas_call(
        tail_kernel,
        out_shape=[jax.ShapeDtypeStruct((2, WINDOW, w), BF16) for w in (kept, cols - kept)],
        grid=(WINDOW // step,),
        in_specs=[spec, spec],
        out_specs=[pl.BlockSpec((2, step, w), lambda i: (0, i, 0)) for w in (kept, cols - kept)],
        compiler_params=pltpu.CompilerParams(dimension_semantics=("arbitrary",)),
        cost_estimate=pl.CostEstimate(flops=0, bytes_accessed=8 * WINDOW * cols, transcendentals=0),
    )(keys, values)


def moved_shard(weight, term):
    moved = weight + term
    target = jnp.sqrt(jnp.sum(weight * weight, axis=0, keepdims=True))
    return moved * (target / jnp.sqrt(jnp.sum(moved * moved, axis=0, keepdims=True) + EPSILON))


def renew_first_kernel(pos_ref, own_ref, far_ref, g_ref, u_ref, d_ref, w_out, bf_out):
    near = pos_ref[1] == 0
    for m, w_ref in enumerate((g_ref, u_ref, d_ref)):
        term = jnp.where(near, own_ref[m].astype(F32), far_ref[m].astype(F32))
        new = moved_shard(w_ref[0], term)
        w_out[m] = new
        bf_out[m] = new.astype(BF16)


def renew_first(pos, head, own, far, gate, up, down):
    _, hw, width = own.shape
    whole = pl.BlockSpec((3, hw, width), lambda i, p: (0, 0, 0))
    shard = pl.BlockSpec((1, hw, width), lambda i, p: (head, 0, p[0]))
    return pl.pallas_call(
        renew_first_kernel,
        out_shape=[jax.ShapeDtypeStruct(own.shape, F32), jax.ShapeDtypeStruct(own.shape, BF16)],
        grid_spec=pltpu.PrefetchScalarGridSpec(
            num_scalar_prefetch=1,
            grid=(1,),
            in_specs=[whole, whole, shard, shard, shard],
            out_specs=[whole, whole],
        ),
        cost_estimate=pl.CostEstimate(flops=18 * hw * width, bytes_accessed=40 * hw * width, transcendentals=0),
    )(pos, own, far, gate, up, down)


def renew_second_kernel(pos_ref, *refs):
    term_refs, w_ref, bf_out = refs[:-2], refs[-2], refs[-1]
    near = pos_ref[1] == 0
    for m in range(3):
        term = term_refs[0][m].astype(F32)
        for other in term_refs[1:]:
            term += other[m].astype(F32)
        weight = w_ref[m]
        bf_out[m] = jnp.where(near, weight, moved_shard(weight, term)).astype(BF16)


def renew_second(pos, terms, weight):
    _, hw, width = weight.shape
    whole = pl.BlockSpec((3, hw, width), lambda i, p: (0, 0, 0))
    return pl.pallas_call(
        renew_second_kernel,
        out_shape=jax.ShapeDtypeStruct(weight.shape, BF16),
        grid_spec=pltpu.PrefetchScalarGridSpec(
            num_scalar_prefetch=1, grid=(1,), in_specs=[whole] * (len(terms) + 1), out_specs=whole
        ),
        cost_estimate=pl.CostEstimate(flops=24 * hw * width, bytes_accessed=40 * hw * width, transcendentals=0),
    )(pos, *terms, weight)


def attend_tile(q, keys, values, outside, half):
    scores = [dot(q, k, ((1,), (1,))) for k in keys]
    scores = [jnp.where(out, F32(-1e30), s) if out is not None else s for s, out in zip(scores, outside)]
    row = lax.broadcasted_iota(jnp.int32, (half, half), 0)
    col = lax.broadcasted_iota(jnp.int32, (half, half), 1)
    own = col <= row
    edge = jnp.where(own, scores[2], scores[0])
    top = jnp.maximum(jnp.max(edge, axis=-1, keepdims=True), jnp.max(scores[1], axis=-1, keepdims=True))
    factor = F32(math.log2(math.e) / math.sqrt(AH))
    p_edge = jnp.exp2((edge - top) * factor)
    p_mid = jnp.exp2((scores[1] - top) * factor)
    total = jnp.sum(p_edge, axis=-1, keepdims=True) + jnp.sum(p_mid, axis=-1, keepdims=True)
    zero = jnp.zeros_like(p_edge)
    probs = [jnp.where(own, zero, p_edge), p_mid, jnp.where(own, p_edge, zero)]
    out = sum(dot(p.astype(BF16), v) for p, v in zip(probs, values))
    return (out * (1.0 / total)).astype(BF16)


def inner_kernel(q_ref, k_ref, v_ref, _, o_ref):
    half = WINDOW // 2
    for t in range(o_ref.shape[0] // half):
        keys = [k_ref[(t + j) * half : (t + j + 1) * half, :] for j in range(3)]
        values = [v_ref[(t + j) * half : (t + j + 1) * half, :] for j in range(3)]
        q = q_ref[(t + 2) * half : (t + 3) * half, :]
        o_ref[t * half : (t + 1) * half, :] = attend_tile(q, keys, values, (None, None, None), half)


def inner_attention(queries, keys, values, first, count, after):
    rows = queries.shape[0]
    strip = pl.BlockSpec((rows, AH), lambda a: (0, first + a))
    return pl.pallas_call(
        inner_kernel,
        out_shape=jax.ShapeDtypeStruct((rows - WINDOW, count * AH), BF16),
        grid=(count,),
        in_specs=[strip] * 3 + [pl.BlockSpec(memory_space=pl.ANY)],
        out_specs=pl.BlockSpec((rows - WINDOW, AH), lambda a: (0, a)),
        compiler_params=pltpu.CompilerParams(dimension_semantics=("arbitrary",)),
        cost_estimate=pl.CostEstimate(
            flops=count * rows * WINDOW * AH * 6,
            bytes_accessed=count * rows * AH * 10,
            transcendentals=count * rows * WINDOW,
        ),
    )(queries, keys, values, after)


def edge_kernel(side, kept, pos_ref, q_ref, k_ref, v_ref, main_ref, rest_ref, relay_ref, *refs):
    o_ref = refs[-1]
    half = WINDOW // 2
    active = pos_ref[1] == side

    @pl.when(active)
    def _():
        first = pos_ref[2] == 0
        rest = jnp.where(pos_ref[0] == 0, relay_ref[...], rest_ref[...])
        halo = jnp.where(pl.program_id(0) < kept, main_ref[...], rest)
        keys = [halo[0, :half], halo[0, half:], k_ref[:half, :], k_ref[half:, :]]
        values = [halo[1, :half], halo[1, half:], v_ref[:half, :], v_ref[half:, :]]
        for t in range(2):
            outside = [first if j + t < 2 else None for j in range(3)]
            o_ref[t * half : (t + 1) * half, :] = attend_tile(
                q_ref[t * half : (t + 1) * half, :], keys[t : t + 3], values[t : t + 3], outside, half
            )

    @pl.when(jnp.logical_not(active))
    def _():
        o_ref[...] = refs[0][...] if len(refs) > 1 else jnp.zeros_like(o_ref)


def edge_attention(pos, queries, keys, values, main, rest, relay, before, side):
    count = queries.shape[1] // AH
    kept = main.shape[-1] // AH
    strip = pl.BlockSpec((WINDOW, AH), lambda a, p: (0, jnp.where(p[1] == side, a, 0)))
    main_spec = pl.BlockSpec(
        (2, WINDOW, AH), lambda a, p: (0, 0, jnp.where(p[1] == side, jnp.minimum(a, kept - 1), 0))
    )
    rest_spec = pl.BlockSpec(
        (2, WINDOW, AH), lambda a, p: (0, 0, jnp.where(p[1] == side, jnp.maximum(a - kept, 0), 0))
    )
    return pl.pallas_call(
        functools.partial(edge_kernel, side, kept),
        out_shape=jax.ShapeDtypeStruct((WINDOW, count * AH), BF16),
        grid_spec=pltpu.PrefetchScalarGridSpec(
            num_scalar_prefetch=1,
            grid=(count,),
            in_specs=[strip, strip, strip, main_spec, rest_spec, rest_spec]
            + [pl.BlockSpec((WINDOW, AH), lambda a, p: (0, 0))] * len(before),
            out_specs=strip,
        ),
        input_output_aliases={7: 0} if before else {},
        compiler_params=pltpu.CompilerParams(dimension_semantics=("arbitrary",)),
        cost_estimate=pl.CostEstimate(
            flops=count * WINDOW * WINDOW * AH * 6,
            bytes_accessed=count * WINDOW * AH * 18,
            transcendentals=count * WINDOW * WINDOW,
        ),
    )(pos, queries, keys, values, main, rest, relay, *before)


def apply_kernel(parts, pos_ref, *refs):
    q_ref, edge_ref, inner_ref = refs[:3]
    pieces = refs[3 : 3 + parts]
    o_ref, w_ref = refs[-2:]
    step = pl.program_id(0)

    @pl.when(step == 0)
    def _():
        gather_weights(pos_ref, pieces, w_ref)

    query_norm = unit_rows(q_ref[...])
    gate_pre = dot(query_norm, w_ref[0])
    up_pre = dot(query_norm, w_ref[1])
    hidden = (gate_pre * sigmoid(gate_pre) * up_pre).astype(BF16)
    fast = dot(hidden, w_ref[2]).astype(BF16).astype(F32)

    @pl.when(step == 0)
    def _():
        o_ref[...] = (fast + edge_ref[...].astype(F32)).astype(BF16)

    @pl.when(step > 0)
    def _():
        o_ref[...] = (fast + inner_ref[...].astype(F32)).astype(BF16)


def apply_fast(pos, head, queries, edge, inner, pieces, before):
    rows, cols = queries.shape
    parts = len(pieces)
    _, hw, width = pieces[0].shape
    in_specs = [
        pl.BlockSpec((WINDOW, hw), lambda i, p: (i, head)),
        pl.BlockSpec((WINDOW, hw), lambda i, p: (0, head)),
        pl.BlockSpec((WINDOW, hw), lambda i, p: (jnp.maximum(i - 1, 0), 0)),
    ] + [pl.BlockSpec((3, hw, width), lambda i, p: (0, 0, 0))] * parts
    operands = [pos, queries, edge, inner, *pieces]
    aliases = {}
    if before is not None:
        in_specs.append(pl.BlockSpec(memory_space=pl.ANY))
        aliases = {len(operands): 0}
        operands.append(before)
    return pl.pallas_call(
        functools.partial(apply_kernel, parts),
        out_shape=jax.ShapeDtypeStruct((rows, cols), BF16),
        grid_spec=pltpu.PrefetchScalarGridSpec(
            num_scalar_prefetch=1,
            grid=(rows // WINDOW,),
            in_specs=in_specs,
            out_specs=pl.BlockSpec((WINDOW, hw), lambda i, p: (i, head)),
            scratch_shapes=[pltpu.VMEM((3, hw, hw), BF16)],
        ),
        input_output_aliases=aliases,
        compiler_params=pltpu.CompilerParams(dimension_semantics=("arbitrary",), vmem_limit_bytes=GRANT),
        cost_estimate=pl.CostEstimate(
            flops=6 * rows * hw * hw, bytes_accessed=8 * rows * hw + 6 * hw * hw, transcendentals=rows * hw
        ),
    )(*operands)


def hop(x, route, axes="seq"):
    return lax.ppermute(x, axes, route)


def spread(xs, low, high):
    rows, cols = lax.axis_size("head"), lax.axis_size("seq")
    got = []
    for d, x in enumerate(xs):
        if d == 0:
            continue
        route = []
        for h in range(rows):
            for i in range(cols):
                if low <= i < high:
                    route.append((h * cols + i, h * cols + (i ^ d)))
                elif rows % 2 == 0:
                    route.append((h * cols + i, (h ^ 1) * cols + i))
        got.append(hop(x, route, ("head", "seq")))
    return got


def fast_device(queries, key_rows, value_rows, learn_rates, gate_fast, down_fast, up_fast):
    heads, hw = gate_fast.shape[:2]
    seq_count = lax.axis_size("seq")
    parts = seq_count // 2
    seq_index = lax.axis_index("seq").astype(jnp.int32)
    pos = jnp.stack([seq_index % parts, seq_index // parts, seq_index])
    early = [(i, i + 1) for i in range(parts - 1, seq_count - 1)]
    late = [(i, i + 1) for i in range(parts - 1)]
    across = [(i, i + parts) for i in range(parts)]
    per_head = hw // AH
    rates = learn_rates.T
    first_w = (gate_fast, up_fast, down_fast)
    span = range(heads)

    count = queries.shape[1] // AH
    main, rest = tail_rows(key_rows, value_rows, (count - count // 4) * AH)
    side_a = hop(rest, [(parts - 1, parts - 2)])
    main_a = hop(main, early)
    rest_a = hop(rest, early[1:])
    relay_a = hop(side_a, [(parts - 2, parts)])
    terms = [grads(pos, h, parts, key_rows, value_rows, rates, first_w, True) for h in span]

    def attend_inner(h, after):
        inner.append(inner_attention(queries, key_rows, value_rows, h * per_head, per_head, after))

    shards, w1, far, inner = [], [], [], []
    for h in span:
        got = spread(terms[h], 0, parts)
        own = terms[h][0].astype(F32)
        for g in got:
            own = own + g.astype(F32)
        own = own.astype(BF16)
        far.append(hop(own, across))
        if h == 0:
            attend_inner(h, own)
        shard, shard_bf = renew_first(pos, h, own, far[h], *first_w)
        shards.append(shard)
        w1.append([shard_bf] + spread([shard_bf] * parts, parts, seq_count))
    edge = edge_attention(pos, queries, key_rows, value_rows, main_a, rest_a, relay_a, (), 1)
    (main, rest), _ = lax.optimization_barrier(((main, rest), own))
    main_b = hop(main, late)
    rest_b = hop(rest, late)
    w2 = []
    for h in span:
        term = grads(pos, h, parts, key_rows, value_rows, rates, w1[h], False)
        got = [term[0]] + spread(term, parts, seq_count)
        shard_bf = renew_second(pos, got, shards[h])
        if h:
            attend_inner(h, w2[h - 1][0])
        w2.append([shard_bf] + spread([shard_bf] * parts, 0, seq_count))
    edge = edge_attention(pos, queries, key_rows, value_rows, main_b, rest_b, rest_b, (edge,), 0)
    out = None
    for h in span:
        out = apply_fast(pos, h, queries, edge, inner[h], w2[h], out)
    return out


def shifted(block, axis, distance):
    devices = range(lax.axis_size(axis))
    route = [(i - distance, i) for i in devices if i - distance in devices]
    return lax.ppermute(block, axis, route)


def norm_rows(values_in, heads_local, head_width):
    as_float = values_in.reshape(values_in.shape[0], heads_local, head_width).astype(jnp.float32)
    return (
        as_float / jnp.sqrt(jnp.mean(as_float * as_float, axis=-1, keepdims=True) + EPSILON)
    ).astype(jnp.bfloat16)


def fast_terms(fast_bf, key_norm, value_heads, rate_rows):
    gate_w, down_w, up_w = fast_bf
    gate_pre = jnp.einsum("nhd,hdf->nhf", key_norm, gate_w, preferred_element_type=jnp.float32)
    up_pre = jnp.einsum("nhd,hdf->nhf", key_norm, up_w, preferred_element_type=jnp.float32)
    sigmoid_gate = jax.nn.sigmoid(gate_pre)
    gate_act = gate_pre * sigmoid_gate
    hidden = (gate_act * up_pre).astype(jnp.bfloat16)
    scaled_val = (
        rate_rows.astype(jnp.float32)[:, :, None] * value_heads.astype(jnp.float32)
    ).astype(jnp.bfloat16)
    hidden_grad = -jnp.einsum(
        "nhe,hfe->nhf", scaled_val, down_w, preferred_element_type=jnp.float32
    )
    gate_grad = (
        hidden_grad * up_pre * sigmoid_gate * (1.0 + gate_pre * (1.0 - sigmoid_gate))
    ).astype(jnp.bfloat16)
    up_grad = (hidden_grad * gate_act).astype(jnp.bfloat16)
    gate_term = jnp.einsum("nhd,nhf->hdf", key_norm, gate_grad, preferred_element_type=jnp.float32)
    down_term = -jnp.einsum("nhf,nhe->hfe", hidden, scaled_val, preferred_element_type=jnp.float32)
    up_term = jnp.einsum("nhd,nhf->hdf", key_norm, up_grad, preferred_element_type=jnp.float32)
    return (gate_term, down_term, up_term)


def rescale(weight, moved):
    target_norm = jnp.sqrt(jnp.sum(weight * weight, axis=-2, keepdims=True))
    return moved * target_norm / jnp.sqrt(jnp.sum(moved * moved, axis=-2, keepdims=True) + EPSILON)


def general_apply(fast_bf, query_norm):
    gate_w, down_w, up_w = fast_bf
    gate_pre = jnp.einsum("nhd,hdf->nhf", query_norm, gate_w, preferred_element_type=jnp.float32)
    up_pre = jnp.einsum("nhd,hdf->nhf", query_norm, up_w, preferred_element_type=jnp.float32)
    hidden = (gate_pre * jax.nn.sigmoid(gate_pre) * up_pre).astype(jnp.bfloat16)
    return jnp.einsum("nhf,hfe->nhe", hidden, down_w, preferred_element_type=jnp.float32).astype(
        jnp.bfloat16
    )


def renew(fast_f32, grad_terms):
    grad_sums = lax.psum((grad_terms[0], grad_terms[1], grad_terms[2]), "seq")
    renewed = tuple(
        (rescale(weight, weight - summed) for weight, summed in zip(fast_f32, grad_sums))
    )
    renewed_bf = tuple((weight.astype(jnp.bfloat16) for weight in renewed))
    return (renewed, renewed_bf)


def general_device(queries, key_rows, value_rows, learn_rates, gate_fast, down_fast, up_fast):
    heads_local = gate_fast.shape[0]
    head_width = gate_fast.shape[1]
    seq_count = lax.axis_size("seq")
    seq_index = lax.axis_index("seq")
    rows_here = queries.shape[0]
    width_here = queries.shape[1]
    fast_f32 = (gate_fast, down_fast, up_fast)
    first_bf = tuple((weight.astype(jnp.bfloat16) for weight in fast_f32))
    own_group = (seq_index >= seq_count // 2).astype(jnp.int32)
    query_norm = norm_rows(queries, heads_local, head_width)
    key_norm = norm_rows(key_rows, heads_local, head_width)
    value_heads = value_rows.reshape(rows_here, heads_local, head_width)
    fast_bf = first_bf
    kept = []
    for group in range(2):
        group_rates = jnp.where(own_group == group, learn_rates, jnp.zeros_like(learn_rates))
        grad_terms = fast_terms(fast_bf, key_norm, value_heads, group_rates)
        fast_f32, fast_bf = renew(fast_f32, grad_terms)
        kept.append(fast_bf)
    chosen = tuple(
        (jnp.where(own_group == 0, early, later) for early, later in zip(kept[0], kept[1]))
    )
    fast_out = general_apply(chosen, query_norm).reshape(rows_here, width_here)
    attn_heads = width_here // AH
    score_scale = 1.0 / math.sqrt(AH)
    prev_keys, prev_values = shifted(
        (key_rows[rows_here - WINDOW :], value_rows[rows_here - WINDOW :]), "seq", 1
    )
    wide_keys = jnp.concatenate([prev_keys, key_rows], axis=0)
    wide_values = jnp.concatenate([prev_values, value_rows], axis=0)
    query_offset = jnp.arange(WINDOW, dtype=jnp.int32)[:, None]
    key_offset = jnp.arange(2 * WINDOW, dtype=jnp.int32)[None, :]
    block_outs = []
    for block in range(rows_here // WINDOW):
        lower = block * WINDOW
        start = seq_index * rows_here + lower
        query_block = queries[lower : lower + WINDOW].reshape(WINDOW, attn_heads, AH)
        key_block = wide_keys[lower : lower + 2 * WINDOW].reshape(2 * WINDOW, attn_heads, AH)
        value_block = wide_values[lower : lower + 2 * WINDOW].reshape(2 * WINDOW, attn_heads, AH)
        scores = (
            jnp.einsum("qhd,khd->hqk", query_block, key_block, preferred_element_type=jnp.float32)
            * score_scale
        )
        query_pos = start + query_offset
        key_pos = start - WINDOW + key_offset
        allowed = (key_pos <= query_pos) & (key_pos > query_pos - WINDOW) & (key_pos >= 0)
        scores = jnp.where(allowed[None], scores, jnp.float32(-1e30))
        top_score = jnp.max(scores, axis=-1, keepdims=True)
        expo = jnp.exp(scores - top_score)
        attend = (expo / jnp.sum(expo, axis=-1, keepdims=True)).astype(jnp.bfloat16)
        block_outs.append(
            jnp.einsum(
                "hqk,khd->qhd", attend, value_block, preferred_element_type=jnp.float32
            ).reshape(WINDOW, width_here)
        )
    attended = jnp.concatenate(block_outs, axis=0)
    return (fast_out.astype(jnp.float32) + attended).astype(jnp.bfloat16)


def solution(mesh):
    parts = mesh.shape["seq"] // 2

    def fits(args):
        width = args[4].shape[1] // parts
        return (
            parts & (parts - 1) == 0
            and parts > 1
            and width % AH == 0
            and args[0].shape[0] >= 2 * WINDOW
            and args[0].shape[1] >= 4 * AH
        )

    def on_device(*args):
        if fits(args):
            return fast_device(*args)
        return general_device(*args)

    return jax.shard_map(
        on_device,
        mesh=mesh,
        in_specs=(
            P("seq", "head"),
            P("seq", "head"),
            P("seq", "head"),
            P("seq", "head"),
            P("head", None, None),
            P("head", None, None),
            P("head", None, None),
        ),
        out_specs=P("seq", "head"),
        check_vma=False,
    )
```

```python
import functools
import math

import jax
import jax.numpy as jnp
from jax import lax
from jax.experimental import pallas as pl
from jax.experimental.pallas import tpu as pltpu
from jax.sharding import PartitionSpec as P


AH = 128
WINDOW = 512
EPSILON = 1e-06
GRANT = 28 * 2**20
F32 = jnp.float32
BF16 = jnp.bfloat16


def dot(a, b, dims=((1,), (0,))):
    return lax.dot_general(a, b, (dims, ((), ())), preferred_element_type=F32)


def unit_rows(x):
    x = x.astype(F32)
    return (x * lax.rsqrt(jnp.mean(x * x, axis=-1, keepdims=True) + EPSILON)).astype(BF16)


def sigmoid(x):
    return 0.5 * jnp.tanh(0.5 * x) + 0.5


def block_of(pos_ref, d, width):
    return pl.ds(pl.multiple_of(jnp.bitwise_xor(pos_ref[0], d) * width, width), width)


def gather_weights(pos_ref, piece_refs, w_ref):
    width = piece_refs[0].shape[-1]
    for d, piece in enumerate(piece_refs):
        for m in range(3):
            w_ref[m, :, block_of(pos_ref, d, width)] = piece[m]


def grads_kernel(parts, whole, head, pos_ref, *refs):
    n_w = 3 if whole else parts
    k_ref, v_ref, r_ref = refs[:3]
    w_in = refs[3 : 3 + n_w]
    outs = refs[3 + n_w : 3 + n_w + parts]
    w_ref, acc_ref = refs[-2:]
    step = pl.program_id(0)

    @pl.when(step == 0)
    def _():
        if whole:
            for m in range(3):
                w_ref[m] = w_in[m][0].astype(BF16)
        else:
            gather_weights(pos_ref, w_in, w_ref)
        acc_ref[...] = jnp.zeros_like(acc_ref)

    key_norm = unit_rows(k_ref[...])
    rate = jnp.transpose(jnp.broadcast_to(r_ref[head : head + 1, :].astype(F32), (8, r_ref.shape[1])))[:, :1]
    scaled = (rate * v_ref[...].astype(F32)).astype(BF16)
    gate_pre = dot(key_norm, w_ref[0])
    up_pre = dot(key_norm, w_ref[1])
    grad = dot(scaled, w_ref[2], ((1,), (1,)))
    sig = sigmoid(gate_pre)
    act = gate_pre * sig
    hidden = (act * up_pre).astype(BF16)
    gate_grad = (grad * up_pre * (sig + act * (1.0 - sig))).astype(BF16)
    up_grad = (grad * act).astype(BF16)
    over_rows = ((0,), (0,))
    acc_ref[0] += dot(key_norm, gate_grad, over_rows)
    acc_ref[1] += dot(key_norm, up_grad, over_rows)
    acc_ref[2] += dot(hidden, scaled, over_rows)

    @pl.when(step == pl.num_programs(0) - 1)
    def _():
        width = outs[0].shape[-1]
        for d, out in enumerate(outs):
            for m in range(3):
                out[m] = acc_ref[m, :, block_of(pos_ref, d, width)].astype(BF16)


def grads(pos, head, parts, keys, values, rates, weights, whole, tile=WINDOW):
    rows, hw = keys.shape[0], weights[0].shape[1]
    width = hw // parts
    row_spec = pl.BlockSpec((tile, hw), lambda i, p: (i, head))
    if whole:
        w_specs = [pl.BlockSpec((1, hw, hw), lambda i, p: (head, 0, 0))] * 3
    else:
        w_specs = [pl.BlockSpec((3, hw, width), lambda i, p: (0, 0, 0))] * parts
    return pl.pallas_call(
        functools.partial(grads_kernel, parts, whole, head),
        out_shape=[jax.ShapeDtypeStruct((3, hw, width), BF16)] * parts,
        grid_spec=pltpu.PrefetchScalarGridSpec(
            num_scalar_prefetch=1,
            grid=(rows // tile,),
            in_specs=[row_spec, row_spec, pl.BlockSpec((rates.shape[0], tile), lambda i, p: (0, i))]
            + w_specs,
            out_specs=[pl.BlockSpec((3, hw, width), lambda i, p: (0, 0, 0))] * parts,
            scratch_shapes=[pltpu.VMEM((3, hw, hw), BF16), pltpu.VMEM((3, hw, hw), F32)],
        ),
        compiler_params=pltpu.CompilerParams(dimension_semantics=("arbitrary",)),
        cost_estimate=pl.CostEstimate(
            flops=12 * rows * hw * hw,
            bytes_accessed=4 * rows * hw + 12 * hw * hw,
            transcendentals=rows * hw,
        ),
    )(pos, keys, values, rates, *weights)


def tail_kernel(k_ref, v_ref, main_ref, rest_ref):
    cut = main_ref.shape[-1]
    for m, ref in enumerate((k_ref, v_ref)):
        main_ref[m] = ref[:, :cut]
        rest_ref[m] = ref[:, cut:]


def tail_rows(keys, values, kept, step=256):
    rows, cols = keys.shape
    first = (rows - WINDOW) // step
    spec = pl.BlockSpec((step, cols), lambda i: (first + i, 0))
    return pl.pallas_call(
        tail_kernel,
        out_shape=[jax.ShapeDtypeStruct((2, WINDOW, w), BF16) for w in (kept, cols - kept)],
        grid=(WINDOW // step,),
        in_specs=[spec, spec],
        out_specs=[pl.BlockSpec((2, step, w), lambda i: (0, i, 0)) for w in (kept, cols - kept)],
        compiler_params=pltpu.CompilerParams(dimension_semantics=("arbitrary",)),
        cost_estimate=pl.CostEstimate(flops=0, bytes_accessed=8 * WINDOW * cols, transcendentals=0),
    )(keys, values)


def moved_shard(weight, term):
    moved = weight + term
    target = jnp.sqrt(jnp.sum(weight * weight, axis=0, keepdims=True))
    return moved * (target / jnp.sqrt(jnp.sum(moved * moved, axis=0, keepdims=True) + EPSILON))


def renew_first_kernel(pos_ref, own_ref, far_ref, g_ref, u_ref, d_ref, w_out, bf_out):
    near = pos_ref[1] == 0
    for m, w_ref in enumerate((g_ref, u_ref, d_ref)):
        term = jnp.where(near, own_ref[m].astype(F32), far_ref[m].astype(F32))
        new = moved_shard(w_ref[0], term)
        w_out[m] = new
        bf_out[m] = new.astype(BF16)


def renew_first(pos, head, own, far, gate, up, down):
    _, hw, width = own.shape
    whole = pl.BlockSpec((3, hw, width), lambda i, p: (0, 0, 0))
    shard = pl.BlockSpec((1, hw, width), lambda i, p: (head, 0, p[0]))
    return pl.pallas_call(
        renew_first_kernel,
        out_shape=[jax.ShapeDtypeStruct(own.shape, F32), jax.ShapeDtypeStruct(own.shape, BF16)],
        grid_spec=pltpu.PrefetchScalarGridSpec(
            num_scalar_prefetch=1,
            grid=(1,),
            in_specs=[whole, whole, shard, shard, shard],
            out_specs=[whole, whole],
        ),
        cost_estimate=pl.CostEstimate(flops=18 * hw * width, bytes_accessed=40 * hw * width, transcendentals=0),
    )(pos, own, far, gate, up, down)


def renew_second_kernel(pos_ref, *refs):
    term_refs, w_ref, bf_out = refs[:-2], refs[-2], refs[-1]
    near = pos_ref[1] == 0
    for m in range(3):
        term = term_refs[0][m].astype(F32)
        for other in term_refs[1:]:
            term += other[m].astype(F32)
        weight = w_ref[m]
        bf_out[m] = jnp.where(near, weight, moved_shard(weight, term)).astype(BF16)


def renew_second(pos, terms, weight):
    _, hw, width = weight.shape
    whole = pl.BlockSpec((3, hw, width), lambda i, p: (0, 0, 0))
    return pl.pallas_call(
        renew_second_kernel,
        out_shape=jax.ShapeDtypeStruct(weight.shape, BF16),
        grid_spec=pltpu.PrefetchScalarGridSpec(
            num_scalar_prefetch=1, grid=(1,), in_specs=[whole] * (len(terms) + 1), out_specs=whole
        ),
        cost_estimate=pl.CostEstimate(flops=24 * hw * width, bytes_accessed=40 * hw * width, transcendentals=0),
    )(pos, *terms, weight)


def attend_tile(q, keys, values, outside, half):
    scores = [dot(q, k, ((1,), (1,))) for k in keys]
    scores = [jnp.where(out, F32(-1e30), s) if out is not None else s for s, out in zip(scores, outside)]
    row = lax.broadcasted_iota(jnp.int32, (half, half), 0)
    col = lax.broadcasted_iota(jnp.int32, (half, half), 1)
    own = col <= row
    edge = jnp.where(own, scores[2], scores[0])
    top = jnp.maximum(jnp.max(edge, axis=-1, keepdims=True), jnp.max(scores[1], axis=-1, keepdims=True))
    factor = F32(math.log2(math.e) / math.sqrt(AH))
    p_edge = jnp.exp2((edge - top) * factor)
    p_mid = jnp.exp2((scores[1] - top) * factor)
    total = jnp.sum(p_edge, axis=-1, keepdims=True) + jnp.sum(p_mid, axis=-1, keepdims=True)
    zero = jnp.zeros_like(p_edge)
    probs = [jnp.where(own, zero, p_edge), p_mid, jnp.where(own, p_edge, zero)]
    out = sum(dot(p.astype(BF16), v) for p, v in zip(probs, values))
    return (out * (1.0 / total)).astype(BF16)


def inner_kernel(q_ref, k_ref, v_ref, _, o_ref):
    half = WINDOW // 2
    for t in range(o_ref.shape[0] // half):
        keys = [k_ref[(t + j) * half : (t + j + 1) * half, :] for j in range(3)]
        values = [v_ref[(t + j) * half : (t + j + 1) * half, :] for j in range(3)]
        q = q_ref[(t + 2) * half : (t + 3) * half, :]
        o_ref[t * half : (t + 1) * half, :] = attend_tile(q, keys, values, (None, None, None), half)


def inner_attention(queries, keys, values, first, count, after):
    rows = queries.shape[0]
    strip = pl.BlockSpec((rows, AH), lambda a: (0, first + a))
    return pl.pallas_call(
        inner_kernel,
        out_shape=jax.ShapeDtypeStruct((rows - WINDOW, count * AH), BF16),
        grid=(count,),
        in_specs=[strip] * 3 + [pl.BlockSpec(memory_space=pl.ANY)],
        out_specs=pl.BlockSpec((rows - WINDOW, AH), lambda a: (0, a)),
        compiler_params=pltpu.CompilerParams(dimension_semantics=("arbitrary",)),
        cost_estimate=pl.CostEstimate(
            flops=count * rows * WINDOW * AH * 6,
            bytes_accessed=count * rows * AH * 10,
            transcendentals=count * rows * WINDOW,
        ),
    )(queries, keys, values, after)


def edge_kernel(side, kept, pos_ref, q_ref, k_ref, v_ref, main_ref, rest_ref, relay_ref, *refs):
    o_ref = refs[-1]
    half = WINDOW // 2
    active = pos_ref[1] == side

    @pl.when(active)
    def _():
        first = pos_ref[2] == 0
        rest = jnp.where(pos_ref[0] == 0, relay_ref[...], rest_ref[...])
        halo = jnp.where(pl.program_id(0) < kept, main_ref[...], rest)
        keys = [halo[0, :half], halo[0, half:], k_ref[:half, :], k_ref[half:, :]]
        values = [halo[1, :half], halo[1, half:], v_ref[:half, :], v_ref[half:, :]]
        for t in range(2):
            outside = [first if j + t < 2 else None for j in range(3)]
            o_ref[t * half : (t + 1) * half, :] = attend_tile(
                q_ref[t * half : (t + 1) * half, :], keys[t : t + 3], values[t : t + 3], outside, half
            )

    @pl.when(jnp.logical_not(active))
    def _():
        o_ref[...] = refs[0][...] if len(refs) > 1 else jnp.zeros_like(o_ref)


def edge_attention(pos, queries, keys, values, main, rest, relay, before, side):
    count = queries.shape[1] // AH
    kept = main.shape[-1] // AH
    strip = pl.BlockSpec((WINDOW, AH), lambda a, p: (0, jnp.where(p[1] == side, a, 0)))
    main_spec = pl.BlockSpec(
        (2, WINDOW, AH), lambda a, p: (0, 0, jnp.where(p[1] == side, jnp.minimum(a, kept - 1), 0))
    )
    rest_spec = pl.BlockSpec(
        (2, WINDOW, AH), lambda a, p: (0, 0, jnp.where(p[1] == side, jnp.maximum(a - kept, 0), 0))
    )
    return pl.pallas_call(
        functools.partial(edge_kernel, side, kept),
        out_shape=jax.ShapeDtypeStruct((WINDOW, count * AH), BF16),
        grid_spec=pltpu.PrefetchScalarGridSpec(
            num_scalar_prefetch=1,
            grid=(count,),
            in_specs=[strip, strip, strip, main_spec, rest_spec, rest_spec]
            + [pl.BlockSpec((WINDOW, AH), lambda a, p: (0, 0))] * len(before),
            out_specs=strip,
        ),
        input_output_aliases={7: 0} if before else {},
        compiler_params=pltpu.CompilerParams(dimension_semantics=("arbitrary",)),
        cost_estimate=pl.CostEstimate(
            flops=count * WINDOW * WINDOW * AH * 6,
            bytes_accessed=count * WINDOW * AH * 18,
            transcendentals=count * WINDOW * WINDOW,
        ),
    )(pos, queries, keys, values, main, rest, relay, *before)


def apply_kernel(parts, pos_ref, *refs):
    q_ref, edge_ref, inner_ref = refs[:3]
    pieces = refs[3 : 3 + parts]
    o_ref, w_ref = refs[-2:]
    step = pl.program_id(0)

    @pl.when(step == 0)
    def _():
        gather_weights(pos_ref, pieces, w_ref)

    query_norm = unit_rows(q_ref[...])
    gate_pre = dot(query_norm, w_ref[0])
    up_pre = dot(query_norm, w_ref[1])
    hidden = (gate_pre * sigmoid(gate_pre) * up_pre).astype(BF16)
    fast = dot(hidden, w_ref[2]).astype(BF16).astype(F32)

    @pl.when(step == 0)
    def _():
        o_ref[...] = (fast + edge_ref[...].astype(F32)).astype(BF16)

    @pl.when(step > 0)
    def _():
        o_ref[...] = (fast + inner_ref[...].astype(F32)).astype(BF16)


def apply_fast(pos, head, queries, edge, inner, pieces, before):
    rows, cols = queries.shape
    parts = len(pieces)
    _, hw, width = pieces[0].shape
    in_specs = [
        pl.BlockSpec((WINDOW, hw), lambda i, p: (i, head)),
        pl.BlockSpec((WINDOW, hw), lambda i, p: (0, head)),
        pl.BlockSpec((WINDOW, hw), lambda i, p: (jnp.maximum(i - 1, 0), 0)),
    ] + [pl.BlockSpec((3, hw, width), lambda i, p: (0, 0, 0))] * parts
    operands = [pos, queries, edge, inner, *pieces]
    aliases = {}
    if before is not None:
        in_specs.append(pl.BlockSpec(memory_space=pl.ANY))
        aliases = {len(operands): 0}
        operands.append(before)
    return pl.pallas_call(
        functools.partial(apply_kernel, parts),
        out_shape=jax.ShapeDtypeStruct((rows, cols), BF16),
        grid_spec=pltpu.PrefetchScalarGridSpec(
            num_scalar_prefetch=1,
            grid=(rows // WINDOW,),
            in_specs=in_specs,
            out_specs=pl.BlockSpec((WINDOW, hw), lambda i, p: (i, head)),
            scratch_shapes=[pltpu.VMEM((3, hw, hw), BF16)],
        ),
        input_output_aliases=aliases,
        compiler_params=pltpu.CompilerParams(dimension_semantics=("arbitrary",), vmem_limit_bytes=GRANT),
        cost_estimate=pl.CostEstimate(
            flops=6 * rows * hw * hw, bytes_accessed=8 * rows * hw + 6 * hw * hw, transcendentals=rows * hw
        ),
    )(*operands)


def hop(x, route, axes="seq"):
    return lax.ppermute(x, axes, route)


def trade(x, partner):
    rows, cols = lax.axis_size("head"), lax.axis_size("seq")
    route = []
    for h in range(rows):
        for i in range(cols):
            if i in partner:
                route.append((h * cols + i, h * cols + partner[i]))
            elif rows % 2 == 0:
                route.append((h * cols + i, (h ^ 1) * cols + i))
    return hop(x, route, ("head", "seq"))


def spread(xs, low, high):
    return [trade(x, {i: i ^ d for i in range(low, high)}) for d, x in enumerate(xs) if d]


def fast_device(queries, key_rows, value_rows, learn_rates, gate_fast, down_fast, up_fast):
    heads, hw = gate_fast.shape[:2]
    seq_count = lax.axis_size("seq")
    parts = seq_count // 2
    seq_index = lax.axis_index("seq").astype(jnp.int32)
    pos = jnp.stack([seq_index % parts, seq_index // parts, seq_index])
    early = [(i, i + 1) for i in range(parts - 1, seq_count - 1)]
    late = [(i, i + 1) for i in range(parts - 1)]
    across = [(i, i + parts) for i in range(parts)]
    per_head = hw // AH
    rates = learn_rates.T
    first_w = (gate_fast, up_fast, down_fast)
    span = range(heads)

    count = queries.shape[1] // AH
    main, rest = tail_rows(key_rows, value_rows, (count - count // 4) * AH)
    side_a = trade(rest, {parts - 1: parts - 2, parts - 2: parts - 1})
    main_a = hop(main, early)
    rest_a = hop(rest, early[1:])
    relay_a = trade(side_a, {parts - 2: parts, parts: parts - 2})
    terms = [grads(pos, h, parts, key_rows, value_rows, rates, first_w, True) for h in span]

    def attend_inner(h, after):
        inner.append(inner_attention(queries, key_rows, value_rows, h * per_head, per_head, after))

    shards, w1, far, inner = [], [], [], []
    for h in span:
        got = spread(terms[h], 0, parts)
        own = terms[h][0].astype(F32)
        for g in got:
            own = own + g.astype(F32)
        own = own.astype(BF16)
        far.append(hop(own, across))
        if h == 0:
            attend_inner(h, own)
        shard, shard_bf = renew_first(pos, h, own, far[h], *first_w)
        shards.append(shard)
        w1.append([shard_bf] + spread([shard_bf] * parts, parts, seq_count))
    edge = edge_attention(pos, queries, key_rows, value_rows, main_a, rest_a, relay_a, (), 1)
    (main, rest), _ = lax.optimization_barrier(((main, rest), own))
    main_b = hop(main, late)
    rest_b = hop(rest, late)
    w2 = []
    for h in span:
        term = grads(pos, h, parts, key_rows, value_rows, rates, w1[h], False)
        got = [term[0]] + spread(term, parts, seq_count)
        shard_bf = renew_second(pos, got, shards[h])
        if h:
            attend_inner(h, w2[h - 1][0])
        w2.append([shard_bf] + spread([shard_bf] * parts, 0, seq_count))
    edge = edge_attention(pos, queries, key_rows, value_rows, main_b, rest_b, rest_b, (edge,), 0)
    out = None
    for h in span:
        out = apply_fast(pos, h, queries, edge, inner[h], w2[h], out)
    return out


def shifted(block, axis, distance):
    devices = range(lax.axis_size(axis))
    route = [(i - distance, i) for i in devices if i - distance in devices]
    return lax.ppermute(block, axis, route)


def norm_rows(values_in, heads_local, head_width):
    as_float = values_in.reshape(values_in.shape[0], heads_local, head_width).astype(jnp.float32)
    return (
        as_float / jnp.sqrt(jnp.mean(as_float * as_float, axis=-1, keepdims=True) + EPSILON)
    ).astype(jnp.bfloat16)


def fast_terms(fast_bf, key_norm, value_heads, rate_rows):
    gate_w, down_w, up_w = fast_bf
    gate_pre = jnp.einsum("nhd,hdf->nhf", key_norm, gate_w, preferred_element_type=jnp.float32)
    up_pre = jnp.einsum("nhd,hdf->nhf", key_norm, up_w, preferred_element_type=jnp.float32)
    sigmoid_gate = jax.nn.sigmoid(gate_pre)
    gate_act = gate_pre * sigmoid_gate
    hidden = (gate_act * up_pre).astype(jnp.bfloat16)
    scaled_val = (
        rate_rows.astype(jnp.float32)[:, :, None] * value_heads.astype(jnp.float32)
    ).astype(jnp.bfloat16)
    hidden_grad = -jnp.einsum(
        "nhe,hfe->nhf", scaled_val, down_w, preferred_element_type=jnp.float32
    )
    gate_grad = (
        hidden_grad * up_pre * sigmoid_gate * (1.0 + gate_pre * (1.0 - sigmoid_gate))
    ).astype(jnp.bfloat16)
    up_grad = (hidden_grad * gate_act).astype(jnp.bfloat16)
    gate_term = jnp.einsum("nhd,nhf->hdf", key_norm, gate_grad, preferred_element_type=jnp.float32)
    down_term = -jnp.einsum("nhf,nhe->hfe", hidden, scaled_val, preferred_element_type=jnp.float32)
    up_term = jnp.einsum("nhd,nhf->hdf", key_norm, up_grad, preferred_element_type=jnp.float32)
    return (gate_term, down_term, up_term)


def rescale(weight, moved):
    target_norm = jnp.sqrt(jnp.sum(weight * weight, axis=-2, keepdims=True))
    return moved * target_norm / jnp.sqrt(jnp.sum(moved * moved, axis=-2, keepdims=True) + EPSILON)


def general_apply(fast_bf, query_norm):
    gate_w, down_w, up_w = fast_bf
    gate_pre = jnp.einsum("nhd,hdf->nhf", query_norm, gate_w, preferred_element_type=jnp.float32)
    up_pre = jnp.einsum("nhd,hdf->nhf", query_norm, up_w, preferred_element_type=jnp.float32)
    hidden = (gate_pre * jax.nn.sigmoid(gate_pre) * up_pre).astype(jnp.bfloat16)
    return jnp.einsum("nhf,hfe->nhe", hidden, down_w, preferred_element_type=jnp.float32).astype(
        jnp.bfloat16
    )


def renew(fast_f32, grad_terms):
    grad_sums = lax.psum((grad_terms[0], grad_terms[1], grad_terms[2]), "seq")
    renewed = tuple(
        (rescale(weight, weight - summed) for weight, summed in zip(fast_f32, grad_sums))
    )
    renewed_bf = tuple((weight.astype(jnp.bfloat16) for weight in renewed))
    return (renewed, renewed_bf)


def general_device(queries, key_rows, value_rows, learn_rates, gate_fast, down_fast, up_fast):
    heads_local = gate_fast.shape[0]
    head_width = gate_fast.shape[1]
    seq_count = lax.axis_size("seq")
    seq_index = lax.axis_index("seq")
    rows_here = queries.shape[0]
    width_here = queries.shape[1]
    fast_f32 = (gate_fast, down_fast, up_fast)
    first_bf = tuple((weight.astype(jnp.bfloat16) for weight in fast_f32))
    own_group = (seq_index >= seq_count // 2).astype(jnp.int32)
    query_norm = norm_rows(queries, heads_local, head_width)
    key_norm = norm_rows(key_rows, heads_local, head_width)
    value_heads = value_rows.reshape(rows_here, heads_local, head_width)
    fast_bf = first_bf
    kept = []
    for group in range(2):
        group_rates = jnp.where(own_group == group, learn_rates, jnp.zeros_like(learn_rates))
        grad_terms = fast_terms(fast_bf, key_norm, value_heads, group_rates)
        fast_f32, fast_bf = renew(fast_f32, grad_terms)
        kept.append(fast_bf)
    chosen = tuple(
        (jnp.where(own_group == 0, early, later) for early, later in zip(kept[0], kept[1]))
    )
    fast_out = general_apply(chosen, query_norm).reshape(rows_here, width_here)
    attn_heads = width_here // AH
    score_scale = 1.0 / math.sqrt(AH)
    prev_keys, prev_values = shifted(
        (key_rows[rows_here - WINDOW :], value_rows[rows_here - WINDOW :]), "seq", 1
    )
    wide_keys = jnp.concatenate([prev_keys, key_rows], axis=0)
    wide_values = jnp.concatenate([prev_values, value_rows], axis=0)
    query_offset = jnp.arange(WINDOW, dtype=jnp.int32)[:, None]
    key_offset = jnp.arange(2 * WINDOW, dtype=jnp.int32)[None, :]
    block_outs = []
    for block in range(rows_here // WINDOW):
        lower = block * WINDOW
        start = seq_index * rows_here + lower
        query_block = queries[lower : lower + WINDOW].reshape(WINDOW, attn_heads, AH)
        key_block = wide_keys[lower : lower + 2 * WINDOW].reshape(2 * WINDOW, attn_heads, AH)
        value_block = wide_values[lower : lower + 2 * WINDOW].reshape(2 * WINDOW, attn_heads, AH)
        scores = (
            jnp.einsum("qhd,khd->hqk", query_block, key_block, preferred_element_type=jnp.float32)
            * score_scale
        )
        query_pos = start + query_offset
        key_pos = start - WINDOW + key_offset
        allowed = (key_pos <= query_pos) & (key_pos > query_pos - WINDOW) & (key_pos >= 0)
        scores = jnp.where(allowed[None], scores, jnp.float32(-1e30))
        top_score = jnp.max(scores, axis=-1, keepdims=True)
        expo = jnp.exp(scores - top_score)
        attend = (expo / jnp.sum(expo, axis=-1, keepdims=True)).astype(jnp.bfloat16)
        block_outs.append(
            jnp.einsum(
                "hqk,khd->qhd", attend, value_block, preferred_element_type=jnp.float32
            ).reshape(WINDOW, width_here)
        )
    attended = jnp.concatenate(block_outs, axis=0)
    return (fast_out.astype(jnp.float32) + attended).astype(jnp.bfloat16)


def solution(mesh):
    parts = mesh.shape["seq"] // 2

    def fits(args):
        width = args[4].shape[1] // parts
        return (
            parts & (parts - 1) == 0
            and parts > 1
            and width % AH == 0
            and args[0].shape[0] >= 2 * WINDOW
            and args[0].shape[1] >= 4 * AH
        )

    def on_device(*args):
        if fits(args):
            return fast_device(*args)
        return general_device(*args)

    return jax.shard_map(
        on_device,
        mesh=mesh,
        in_specs=(
            P("seq", "head"),
            P("seq", "head"),
            P("seq", "head"),
            P("seq", "head"),
            P("head", None, None),
            P("head", None, None),
            P("head", None, None),
        ),
        out_specs=P("seq", "head"),
        check_vma=False,
    )
```
